512 devices in a mesh: blk: 32 (over z, core), az: 16 (over y, x).
Axes of the slice: x: 4, y: 4, z: 16, core: 2. Of those that a mesh axis runs over, the one named last changes fastest.
Arguments:
- state: float32 [5, 1024, 128, 128], P(None, 'az', 'blk'), as said below
- cutoffs: int32 [4], replicated, may hold values from 1 to 64, as said below
Outputs:
- advanced: float32 [5, 1024, 128, 128], P(None, 'az', 'blk')
The draws below stay inside these ranges and needn't reach their ends.
Inputs may be any that keep to these rules, and one draw needn't show every extreme that they name: `state`: density lies within 0.5 to 2 and the pressure recovered from the fields is positive at every point. `cutoffs`: some cycle has cutoff 64.
All inputs are finite; a program needn't handle non-finite values.
Results may differ from the reference program's by a relative error of at most 0.0003.
Values sent between devices are 32-bit elements; how exact they have to be, the bound alone decides.
A program may use at most 64 MiB of HBM per device.

```python
import math
import jax
import jax.numpy as jnp
from jax import lax

NTH = 1024
NZ = 128
NEAR = 4
MMAX = 64
NR = 128


def draw_state(key, part):
    keys = jax.random.split(key, 5)
    shape = (NTH, NR, NZ)
    density = jax.random.uniform(keys[0], shape, jnp.float32, 0.6, 1.6)
    radial = 0.2 * jnp.clip(jax.random.normal(keys[1], shape, jnp.float32), -3.0, 3.0)
    swirl = 0.2 * jnp.clip(jax.random.normal(keys[2], shape, jnp.float32), -3.0, 3.0)
    axial = 0.3 * jnp.clip(jax.random.normal(keys[3], shape, jnp.float32), -3.0, 3.0)
    pressure = jax.random.uniform(keys[4], shape, jnp.float32, 0.7, 1.4)
    energy = pressure / 0.4 + 0.5 * density * (radial * radial + swirl * swirl + axial * axial)
    return jnp.stack([density, density * radial, density * swirl, density * axial, energy], 0)


def draw_cutoffs(key, part):
    first, second = jax.random.split(jax.random.fold_in(key, 7))
    values = jax.random.randint(first, (NEAR,), 1, MMAX + 1, jnp.int32)
    where_top = jax.random.randint(second, (), 0, NEAR, jnp.int32)
    return jnp.where(jnp.arange(NEAR, dtype=jnp.int32) == where_top, MMAX, values).astype(jnp.int32)


def setup_inputs(seed: int = 0) -> dict:
    key_of = jax.random.split(jax.random.key(seed), 3)
    return {
        "state": draw_state(jax.random.fold_in(key_of[2], 71), 0),
        "cutoffs": draw_cutoffs(jax.random.fold_in(key_of[2], 71), 0),
    }


gas_factor = 0.4
time_step = 0.025


def primitives(q):
    rho = q[0]
    ur = q[1] / rho
    ut = q[2] / rho
    uz = q[3] / rho
    pressure = gas_factor * (q[4] - 0.5 * (q[1] * ur + q[2] * ut + q[3] * uz))
    return ur, ut, uz, pressure


def flux(q, which):
    ur, ut, uz, pressure = primitives(q)
    speed = [ur, ut, uz][which]
    parts = [q[1 + which], q[1] * speed, q[2] * speed, q[3] * speed, (q[4] + pressure) * speed]
    parts[1 + which] = parts[1 + which] + pressure
    return jnp.stack(parts, 0)


def slope(field, axis):
    count = field.shape[axis]
    def piece(offset):
        return lax.slice_in_dim(field, offset, count - 4 + offset, axis=axis)
    return (piece(0) - 8.0 * piece(1) + 8.0 * piece(3) - piece(4)) / 12.0


def rate(center, theta_pad, cycle_pad, axial_pad, r_mid, r_pad, angle_step):
    radius = r_mid[None, None, :, None]
    radial = slope(r_pad[None, None, :, None] * flux(cycle_pad, 0), 2) / radius
    azimuth = slope(flux(theta_pad, 1), 1) / (angle_step * radius)
    axial = slope(flux(axial_pad, 2), 3)
    ur, ut, uz, pressure = primitives(center)
    zeros = jnp.zeros_like(ut)
    source = jnp.stack([zeros, (center[2] * ut + pressure) / radius[0], -(center[1] * ut) / radius[0], zeros, zeros], 0)
    return source - radial - azimuth - axial


def tables(first, rows, total, modes):
    angles_k = first + jnp.arange(rows, dtype=jnp.int32)
    orders = jnp.arange(modes, dtype=jnp.int32)
    product = (orders[:, None] * angles_k[None, :]) % total
    angle = product.astype(jnp.float32) * (2.0 * math.pi / total)
    return jnp.cos(angle), jnp.sin(angle)


def weights(cutoffs, modes, total):
    orders = jnp.arange(modes, dtype=jnp.int32)
    scale = jnp.where(orders == 0, 1.0, 2.0).astype(jnp.float32) / total
    return jnp.where(orders[:, None] < cutoffs[None, :], scale[:, None], jnp.zeros((), jnp.float32))


def reference(state, cutoffs):
    hi = lax.Precision.HIGHEST
    sign = jnp.array([1.0, -1.0, -1.0, 1.0, 1.0], jnp.float32)[:, None, None, None]
    padded = jnp.pad(state, ((0, 0), (0, 0), (0, 0), (2, 2)), mode="edge")
    r_mid = jnp.arange(NR, dtype=jnp.int32).astype(jnp.float32) + 0.5
    r_pad = (jnp.arange(NR + 4, dtype=jnp.int32) - 2).astype(jnp.float32) + 0.5
    angle_step = 2.0 * math.pi / NTH
    blocks = NZ // 8

    def one_block(index):
        slab = lax.dynamic_slice_in_dim(padded, (index * 8).astype(jnp.int32), 12, axis=3)
        center = slab[..., 2:-2]
        theta_pad = jnp.concatenate([center[:, -2:], center, center[:, :2]], 1)
        lower = jnp.roll(center[:, :, 1::-1], NTH // 2, axis=1) * sign
        upper = jnp.concatenate([center[:, :, -1:], center[:, :, -1:]], 2)
        cycle_pad = jnp.concatenate([lower, center, upper], 2)
        return center + time_step * rate(center, theta_pad, cycle_pad, slab, r_mid, r_pad, angle_step)

    stacked = lax.map(one_block, jnp.arange(blocks, dtype=jnp.int32))
    section = jnp.moveaxis(stacked, 0, 3).reshape(5, NTH, NR, NZ)
    near = section[:, :, :NEAR, :]
    cos_t, sin_t = tables(0, NTH, NTH, MMAX)
    coef_a = jnp.einsum("mk,fkjz->fmjz", cos_t, near, precision=hi)
    coef_b = jnp.einsum("mk,fkjz->fmjz", sin_t, near, precision=hi)
    mode_w = weights(cutoffs, MMAX, NTH)[None, :, :, None]
    kept = jnp.einsum("mk,fmjz->fkjz", cos_t, coef_a * mode_w, precision=hi) + jnp.einsum("mk,fmjz->fkjz", sin_t, coef_b * mode_w, precision=hi)
    return jnp.concatenate([kept, section[:, :, NEAR:, :]], 2)
```

```python
import functools
import math

import jax
import jax.numpy as jnp
import ml_dtypes
import numpy as np
from jax import lax
from jax.experimental import pallas as pl
from jax.experimental.pallas import tpu as pltpu
from jax.sharding import PartitionSpec as P

MESH = pl.DeviceIdType.MESH
FIELDS = 5
MMAX = 64
GAS = 0.4
STEP = 0.025
SIGN = (1.0, -1.0, -1.0, 1.0, 1.0)


def tables(total):
    product = (np.arange(MMAX)[:, None] * np.arange(total)[None, :]) % total
    angle = product * (2.0 * math.pi / total)
    both = np.concatenate([np.cos(angle), np.sin(angle)], 0)
    high = both.astype(ml_dtypes.bfloat16)
    low = (both - high.astype(np.float64)).astype(ml_dtypes.bfloat16)
    return high, low


def axial_matrix(count):
    out = np.zeros((count, count))
    for i in range(count):
        for offset, c in ((-2, 1.0), (-1, -8.0), (1, 8.0), (2, -1.0)):
            out[min(max(i + offset, 0), count - 1), i] += c
    return out.astype(ml_dtypes.bfloat16)


def unit_of(az):
    x = lax.rem(az, 4)
    y = az // 4
    d = lax.rem(x - y + 4, 4)
    upper = d // 2
    odd = lax.rem(d, 2)
    e0 = (1 - upper) * (1 - odd)
    e2 = upper * (1 - odd)
    e3 = upper * odd
    return x + e2 * (4 - x), 2 * e0 + e2 * x + e3


def split(value):
    high = value.astype(jnp.bfloat16)
    return high, (value - high.astype(jnp.float32)).astype(jnp.bfloat16)


def mixed(table_high, table_low, high, low):
    dot = functools.partial(jnp.dot, preferred_element_type=jnp.float32)
    return dot(table_high, high) + (dot(table_high, low) + dot(table_low, high))


def primitives(q):
    inv = 1.0 / q[0]
    ur, ut, uz = q[1] * inv, q[2] * inv, q[3] * inv
    p = GAS * (q[4] - 0.5 * (q[1] * ur + q[2] * ut + q[3] * uz))
    return ur, ut, uz, p


def kernel(blocks, sectors, cut, state, ch_h, cl_h, th_h, tl_h, dz_h, out, u, rf, gs, hh, hl, zd, sb, sg, halo,
           rx, xh, xl, kp, ks, ch, cl, th, tl, dz, load_sem, table_sem, hs, hr, fs, fr, bs, br, own_sem, out_sem):
    blk = lax.axis_index("blk")
    az = lax.axis_index("az")
    first = blk == 0
    last = blk == blocks - 1
    x, y = lax.rem(az, 4), az // 4
    diagonal = x == y
    owner = first | ((blk == 1) & diagonal)
    others = range(1, sectors)

    def at(i):
        return lax.rem(az + i, sectors)

    loads = [pltpu.make_async_copy(state.at[:, :, j], u.at[:, 2 + j], load_sem.at[j]) for j in range(4)]
    for copy in loads:
        copy.start()
    fetch = [
        pltpu.make_async_copy(s, d, table_sem.at[i])
        for i, (s, d) in enumerate(((dz_h, dz), (ch_h, ch), (cl_h, cl), (th_h, th), (tl_h, tl)))
    ]
    fetch[0].start()

    barrier = pltpu.get_barrier_semaphore()

    def greet(b, a):
        pl.semaphore_signal(barrier, inc=1, device_id=(b, a), device_id_type=MESH)

    @pl.when(first)
    def _():
        greet(1, az)
        for i in others:
            greet(0, at(i))
        for k in range(4):
            greet(1, 5 * k)

    @pl.when(blk > 0)
    def _():
        greet(blk - 1, az)
        greet(blk, at(1))
        greet(blk, at(sectors - 1))

        @pl.when(blk < blocks - 1)
        def _():
            greet(blk + 1, az)

    @pl.when((blk == 1) & diagonal)
    def _():
        for i in range(sectors):
            greet(0, at(i))

    @pl.when(owner)
    def _():
        for copy in fetch[1:]:
            copy.start()

    def remote(src, dst, send, recv, b, a):
        return pltpu.make_async_remote_copy(
            src_ref=src, dst_ref=dst, send_sem=send, recv_sem=recv, device_id=(b, a), device_id_type=MESH
        )

    up = remote(u.at[:, 4:6], u.at[:, 0:2], hs.at[0], hr.at[0], jnp.minimum(blk + 1, blocks - 1), az)
    down = remote(u.at[:, 2:4], u.at[:, 6:8], hs.at[1], hr.at[1], jnp.maximum(blk - 1, 0), az)
    ahead = remote(state.at[:, 62:64], halo.at[0], hs.at[2], hr.at[2], blk, at(1))
    behind = remote(state.at[:, 0:2], halo.at[1], hs.at[3], hr.at[3], blk, at(sectors - 1))

    for copy in loads:
        copy.wait()

    @pl.when(blk > 0)
    def _():
        @pl.when((blk == 1) & diagonal)
        def _():
            pl.semaphore_wait(barrier, 4 + sectors)

        @pl.when((blk > 1) & (blk < blocks - 1))
        def _():
            pl.semaphore_wait(barrier, 4)

        @pl.when((blk == 1) & jnp.logical_not(diagonal))
        def _():
            pl.semaphore_wait(barrier, 4)

        @pl.when(last)
        def _():
            pl.semaphore_wait(barrier, 3)

        down.start()

        @pl.when(blk < blocks - 1)
        def _():
            up.start()

        ahead.start()
        behind.start()

    base = (blk * 4).astype(jnp.float32) + 0.5

    def radius(j):
        return base + float(j)

    for j in range(4):
        r = radius(j)
        rate = STEP / r

        def own(i, carry, j=j, r=r, rate=rate):
            rows = pl.ds(pl.multiple_of(i * 16, 16), 16)
            q = [u[f, 2 + j, rows] for f in range(FIELDS)]
            ur, ut, uz, p = primitives(q)
            e = q[4] + p
            cross = q[1] * ut
            swirl = q[2] * ut + p
            radial = [q[1], q[1] * ur + p, cross, q[3] * ur, e * ur]
            azimuth = [q[2], cross, swirl, q[3] * ut, e * ut]
            axial = [q[3], q[1] * uz, q[2] * uz, q[3] * uz + p, e * uz]
            grown = [q[0], q[1] + rate * swirl, q[2] - rate * cross, q[3], q[4]]
            ahead_rows = pl.ds(pl.multiple_of(16 + i * 16, 16), 16)
            for f in range(FIELDS):
                rf[f, 2 + j, rows] = r * radial[f]
                gs[f, j, ahead_rows] = azimuth[f]
                sb[f, j, rows] = grown[f]
                high, low = split(axial[f])
                hh[f, j, rows] = high
                hl[f, j, rows] = low
            return carry

        lax.fori_loop(0, 4, own, 0)

    fetch[0].wait()
    for f in range(FIELDS):
        for j in range(4):
            zd[f, j] = jnp.dot(hh[f, j], dz[...], preferred_element_type=jnp.float32) + jnp.dot(
                hl[f, j], dz[...], preferred_element_type=jnp.float32
            )

    def far_flux(c):
        r = base + float(c - 2)

        def body(i, carry):
            rows = pl.ds(pl.multiple_of(i * 16, 16), 16)
            q = [u[f, c, rows] for f in range(FIELDS)]
            ur, _, _, p = primitives(q)
            radial = [q[1], q[1] * ur + p, q[2] * ur, q[3] * ur, (q[4] + p) * ur]
            for f in range(FIELDS):
                rf[f, c, rows] = r * radial[f]
            return carry

        lax.fori_loop(0, 4, body, 0)

    turn = STEP / (12.0 * 2.0 * math.pi / (64 * sectors))

    def slope_angle(f, j, start, count):
        def part(offset):
            return gs[f, j, start + 16 + offset : start + 16 + offset + count]

        return (part(-2) - part(2)) + 8.0 * (part(1) - part(-1))

    def advance(j):
        kr = (STEP / 12.0) / radius(j)
        kt = turn / radius(j)
        for f in range(FIELDS):
            for h in (0, 32):
                rows = slice(h, h + 32)
                rad = (rf[f, j, rows] - rf[f, j + 4, rows]) + 8.0 * (rf[f, j + 3, rows] - rf[f, j + 1, rows])
                sg[f, j, rows] = (
                    sb[f, j, rows] - kr * rad - kt * slope_angle(f, j, h, 32) - (STEP / 12.0) * zd[f, j, rows]
                )

    def edges(j):
        kt = turn / radius(j)
        for f in range(FIELDS):
            sg[f, j, 64:72] = -kt * (slope_angle(f, j, 64, 8) + slope_angle(f, j, -8, 8))

    def forward(target_blk, target, f, j, rows, slot):
        return remote(sg.at[f, j, 0:rows], rx.at[az, 0:rows], fs.at[slot], fr.at[az], target_blk, target)

    def forward_all(heavy, act):
        for i in others:
            target = at(i)
            f, j = unit_of(target)

            @pl.when((j < 2) if heavy else (j >= 2))
            def _():
                act(forward(0, target, f, j, 136 if heavy else 72, i))

        if not heavy:
            for k in range(4):
                act(forward(1, 5 * k, k, 3, 72, 16 + k))

    my_f, my_j = unit_of(az)
    my_j = jnp.where(first, my_j, 3)
    my_heavy = my_j < 2

    @pl.when(first)
    def _():
        zero = jnp.zeros((64, 128), jnp.float32)
        for f in range(FIELDS):
            for c in range(2):
                rf[f, c] = zero
            for j in range(4):
                gs[f, j, 0:16] = zero[:16]
                gs[f, j, 80:96] = zero[:16]
        for j in range(2):
            advance(j)
            edges(j)
            kr = (STEP / 12.0) / radius(j)
            for f in range(FIELDS):
                inner = rf[f, 3] - 8.0 * rf[f, 2] if j == 0 else rf[f, 2]
                sg[f, j, 72:136] = (-SIGN[f] * kr) * inner
        pl.semaphore_wait(barrier, 4 + sectors)
        forward_all(True, lambda c: c.start())
        up.start()

    @pl.when(blk > 0)
    def _():
        ahead.wait_recv()
        behind.wait_recv()
        for side in range(2):
            for a in range(2):
                q = [halo[side, f, a] for f in range(FIELDS)]
                _, ut, _, p = primitives(q)
                azimuth = [q[2], q[1] * ut, q[2] * ut + p, q[3] * ut, (q[4] + p) * ut]
                row = (14 if side == 0 else 80) + a
                for f in range(FIELDS):
                    for j in range(4):
                        gs[f, j, row : row + 1] = azimuth[f][j : j + 1]
        up.wait_recv()
        for c in range(2):
            far_flux(c)

    @pl.when(last)
    def _():
        for f in range(FIELDS):
            for c in (6, 7):
                u[f, c] = u[f, 5]

    @pl.when(blk < blocks - 1)
    def _():
        down.wait_recv()

    for c in (6, 7):
        far_flux(c)

    def stored(f, j):
        return pltpu.make_async_copy(ks.at[f, j], out.at[f, :, j], out_sem.at[f, j])

    def plain(j):
        return pltpu.make_async_copy(sg.at[:, j, 0:64], out.at[:, :, j], out_sem.at[0, j])

    @pl.when(first)
    def _():
        for j in range(2, 4):
            advance(j)
            edges(j)
        forward_all(False, lambda c: c.start())

    @pl.when(blk > 0)
    def _():
        for j in range(4):
            advance(j)
            plain(j).start()

    def back(i, target):
        return remote(kp.at[target], ks.at[my_f, my_j], bs.at[i], br.at[blk * sectors + az], 0, target)

    @pl.when(owner)
    def _():
        for heavy in (True, False):
            rows = 136 if heavy else 72

            @pl.when(my_heavy if heavy else jnp.logical_not(my_heavy))
            def _(rows=rows):
                @pl.when(first)
                def _():
                    pltpu.make_async_copy(sg.at[my_f, my_j, 0:rows], rx.at[az, 0:rows], own_sem.at[0]).start()

                for i in range(sectors):
                    s = at(i)
                    arrival = remote(sg.at[0, 0, 0:rows], rx.at[s, 0:rows], fs.at[i], fr.at[s], 0, s)
                    if i == 0:
                        pl.when(blk == 1)(arrival.wait_recv)
                    else:
                        arrival.wait_recv()

                @pl.when(first)
                def _():
                    pltpu.make_async_copy(sg.at[my_f, my_j, 0:rows], rx.at[az, 0:rows], own_sem.at[0]).wait()

                edge_row = lax.broadcasted_iota(jnp.int32, (8, 128), 0)

                def gather(s, carry):
                    before = rx[lax.rem(s + sectors - 1, sectors), 64:72]
                    after = rx[lax.rem(s + 1, sectors), 64:72]
                    rx[s, 0:8] = rx[s, 0:8] + jnp.where(edge_row < 4, before, 0.0)
                    rx[s, 56:64] = rx[s, 56:64] + jnp.where(edge_row < 4, 0.0, after)
                    value = rx[s, 0:64]
                    if rows == 136:
                        value = value + rx[lax.rem(s + sectors // 2, sectors), 72:136]
                    high, low = split(value)
                    to = pl.ds(pl.multiple_of(s * 64, 64), 64)
                    xh[to] = high
                    xl[to] = low
                    return carry

                lax.fori_loop(0, sectors, gather, 0)

        for copy in fetch[1:]:
            copy.wait()
        coef = mixed(ch[...], cl[...], xh[...], xl[...])
        order = lax.rem(lax.broadcasted_iota(jnp.int32, (2 * MMAX, 128), 0), MMAX)
        scale = jnp.where(order == 0, 1.0, 2.0) / float(64 * sectors)
        high, low = split(coef * jnp.where(order < cut[my_j], scale, 0.0))
        for n in (2, 1, 3, 0):
            yy = lax.rem(y + n, 4)
            rows = pl.ds(pl.multiple_of(yy * 256, 256), 256)
            kept = mixed(th[rows], tl[rows], high, low)
            for i in range(4):
                s = yy * 4 + i
                kp[s] = kept[64 * i : 64 * i + 64]

                @pl.when(jnp.logical_not(first & (s == az)))
                def _(s=s):
                    back(s, s).start()

        @pl.when(first)
        def _():
            own = pltpu.make_async_copy(kp.at[az], ks.at[my_f, my_j], own_sem.at[0])
            own.start()
            own.wait()

    @pl.when(first)
    def _():
        stored(my_f, my_j).start()
        for i in others:
            o = at(i)
            f, j = unit_of(o)
            remote(kp.at[0], ks.at[f, j], bs.at[0], br.at[o], 0, o).wait_recv()
            stored(f, j).start()
        for k in range(4):
            remote(kp.at[0], ks.at[k, 3], bs.at[0], br.at[sectors + 5 * k], 1, 5 * k).wait_recv()
            stored(k, 3).start()
        for f in range(FIELDS):
            for j in range(4):
                stored(f, j).wait()
        up.wait_send()
        forward_all(True, lambda c: c.wait_send())
        forward_all(False, lambda c: c.wait_send())

    @pl.when(owner)
    def _():
        for s in range(sectors):
            @pl.when(jnp.logical_not(first & (s == az)))
            def _(s=s):
                back(s, s).wait_send()

    @pl.when(blk > 0)
    def _():
        for j in range(4):
            plain(j).wait()
        down.wait_send()

        @pl.when(blk < blocks - 1)
        def _():
            up.wait_send()

        ahead.wait_send()
        behind.wait_send()


def shards(cut_table, blocks, sectors, state, cutoffs):
    high, low = cut_table
    points = state.shape[3]
    f32, bf16 = jnp.float32, jnp.bfloat16
    dma = pltpu.SemaphoreType.DMA
    anywhere = pl.BlockSpec(memory_space=pl.ANY)
    total = 64 * sectors
    return pl.pallas_call(
        functools.partial(kernel, blocks, sectors),
        out_shape=jax.ShapeDtypeStruct(state.shape, f32),
        in_specs=[pl.BlockSpec(memory_space=pltpu.SMEM)] + [anywhere] * 6,
        out_specs=anywhere,
        scratch_shapes=[
            pltpu.VMEM((FIELDS, 8, 64, points), f32),
            pltpu.VMEM((FIELDS, 8, 64, points), f32),
            pltpu.VMEM((FIELDS, 4, 96, points), f32),
            pltpu.VMEM((FIELDS, 4, 64, points), bf16),
            pltpu.VMEM((FIELDS, 4, 64, points), bf16),
            pltpu.VMEM((FIELDS, 4, 64, points), f32),
            pltpu.VMEM((FIELDS, 4, 64, points), f32),
            pltpu.VMEM((FIELDS, 4, 136, points), f32),
            pltpu.VMEM((2, FIELDS, 2, 4, points), f32),
            pltpu.VMEM((sectors, 136, points), f32),
            pltpu.VMEM((total, points), bf16),
            pltpu.VMEM((total, points), bf16),
            pltpu.VMEM((sectors, 64, points), f32),
            pltpu.VMEM((FIELDS, 4, 64, points), f32),
            pltpu.VMEM((2 * MMAX, total), bf16),
            pltpu.VMEM((2 * MMAX, total), bf16),
            pltpu.VMEM((total, 2 * MMAX), bf16),
            pltpu.VMEM((total, 2 * MMAX), bf16),
            pltpu.VMEM((points, points), bf16),
            dma((4,)),
            dma((5,)),
            dma((4,)),
            dma((4,)),
            dma((20,)),
            dma((sectors,)),
            dma((sectors,)),
            dma((2 * sectors,)),
            dma((1,)),
            dma((FIELDS, 4)),
        ],
        compiler_params=pltpu.CompilerParams(
            collective_id=0, has_side_effects=True, vmem_limit_bytes=60 * 1024 * 1024
        ),
        name="section",
    )(
        cutoffs,
        state,
        jnp.asarray(high),
        jnp.asarray(low),
        jnp.asarray(np.ascontiguousarray(high.T)),
        jnp.asarray(np.ascontiguousarray(low.T)),
        jnp.asarray(axial_matrix(points)),
    )


def solution(mesh):
    blocks, sectors = mesh.shape["blk"], mesh.shape["az"]
    placed = (P(None, "az", "blk", None), P())
    return jax.shard_map(
        functools.partial(shards, tables(64 * sectors), blocks, sectors),
        mesh=mesh,
        in_specs=placed,
        out_specs=P(None, "az", "blk", None),
        check_vma=False,
    )
```

```python
import functools
import math

import jax
import jax.numpy as jnp
import ml_dtypes
import numpy as np
from jax import lax
from jax.experimental import pallas as pl
from jax.experimental.pallas import tpu as pltpu
from jax.sharding import PartitionSpec as P

MESH = pl.DeviceIdType.MESH
FIELDS = 5
MMAX = 64
GAS = 0.4
STEP = 0.025
SIGN = (1.0, -1.0, -1.0, 1.0, 1.0)
LIMIT_MIB = 53


OFFSETS = sorted(
    ((dx, dy) for dx in range(4) for dy in range(4) if dx or dy),
    key=lambda o: -(min(o[0], 4 - o[0]) + min(o[1], 4 - o[1])),
)


def tables(total):
    product = (np.arange(MMAX)[:, None] * np.arange(total)[None, :]) % total
    angle = product * (2.0 * math.pi / total)
    both = np.concatenate([np.cos(angle), np.sin(angle)], 0)
    high = both.astype(ml_dtypes.bfloat16)
    low = (both - high.astype(np.float64)).astype(ml_dtypes.bfloat16)
    parts = np.concatenate([high, low], 0)
    blocked = parts.reshape(4 * MMAX, total // 64, 4, 16).transpose(2, 0, 1, 3).reshape(total, 256)
    return np.stack([blocked, parts.T])


def units_of(az):
    t = lax.rem(az + az // 4, 4)
    odd, upper = lax.rem(t, 2), t // 2
    return az // 4, 2 * odd + upper, 2 * (1 - odd) + upper


def exchanged(pieces):
    group = lax.broadcasted_iota(jnp.int32, pieces[0].shape, 1) // 32
    out = []
    for a in range(4):
        value = pieces[a]
        for b in range(4):
            if b != a:
                value = jnp.where(group == b, pltpu.roll(pieces[b], (32 * (b - a)) % 128, 1), value)
        out.append(value)
    return out


def split(value):
    high = value.astype(jnp.bfloat16)
    return high, (value - high.astype(jnp.float32)).astype(jnp.bfloat16)


def product(a, b):
    return jnp.dot(a, b, preferred_element_type=jnp.float32)


def axial_matrix():
    point = lax.rem(lax.broadcasted_iota(jnp.int32, (256, 128), 0), 128)
    at = lax.broadcasted_iota(jnp.int32, (256, 128), 1)
    total = jnp.zeros((256, 128), jnp.float32)
    for offset, c in ((-2, 1.0), (-1, -8.0), (1, 8.0), (2, -1.0)):
        total = total + jnp.where(point == jnp.clip(at + offset, 0, 127), c, 0.0)
    return total.astype(jnp.bfloat16)


def primitives(q):
    inv = 1.0 / q[0]
    ur, ut, uz = q[1] * inv, q[2] * inv, q[3] * inv
    p = GAS * (q[4] - 0.5 * (q[1] * ur + q[2] * ut + q[3] * uz))
    return ur, ut, uz, p


def kernel(blocks, sectors, cut, state, transforms, out, u, rf, gs, hh, zd, sb, sg, halo,
           rx, rq, pk, xs, kp, kq, qin, o4, tt, dz, load_sem, table_sem, hs, hr, fs, fr, bs, br, own_sem, out_sem):
    blk = lax.axis_index("blk")
    az = lax.axis_index("az")
    first = blk == 0
    last = blk == blocks - 1
    x, y = lax.rem(az, 4), az // 4
    others = range(1, sectors)

    def at(i):
        return lax.rem(az + i, sectors)

    loads = [pltpu.make_async_copy(state.at[:, :, j], u.at[:, 2 + j], load_sem.at[j]) for j in range(4)]
    for copy in loads:
        copy.start()
    fetch = pltpu.make_async_copy(transforms, tt, table_sem.at[0])

    barrier = pltpu.get_barrier_semaphore()

    def greet(b, a):
        pl.semaphore_signal(barrier, inc=1, device_id=(b, a), device_id_type=MESH)

    @pl.when(first)
    def _():
        greet(1, az)
        for i in others:
            greet(0, at(i))
        fetch.start()

    @pl.when(blk > 0)
    def _():
        greet(blk - 1, az)
        greet(blk, at(1))
        greet(blk, at(sectors - 1))

        @pl.when(blk < blocks - 1)
        def _():
            greet(blk + 1, az)

    def remote(src, dst, send, recv, b, a):
        return pltpu.make_async_remote_copy(
            src_ref=src, dst_ref=dst, send_sem=send, recv_sem=recv, device_id=(b, a), device_id_type=MESH
        )

    up = remote(u.at[:, 4:6], u.at[:, 0:2], hs.at[0], hr.at[0], jnp.minimum(blk + 1, blocks - 1), az)
    down = remote(u.at[:, 2:4], u.at[:, 6:8], hs.at[1], hr.at[1], jnp.maximum(blk - 1, 0), az)
    ahead = remote(state.at[:, 62:64], halo.at[0], hs.at[2], hr.at[2], blk, at(1))
    behind = remote(state.at[:, 0:2], halo.at[1], hs.at[3], hr.at[3], blk, at(sectors - 1))

    dz[...] = axial_matrix()

    @pl.when(first)
    def _():
        zero = jnp.zeros((64, 128), jnp.float32)
        for f in range(FIELDS):
            for c in range(2):
                rf[f, c] = zero
            for j in range(4):
                gs[f, j, 0:16] = zero[:16]
                gs[f, j, 80:96] = zero[:16]

    for copy in loads:
        copy.wait()

    @pl.when(blk > 0)
    def _():
        @pl.when(blk < blocks - 1)
        def _():
            pl.semaphore_wait(barrier, 4)

        @pl.when(last)
        def _():
            pl.semaphore_wait(barrier, 3)

        down.start()

        @pl.when(blk < blocks - 1)
        def _():
            up.start()

        ahead.start()
        behind.start()

    base = (blk * 4).astype(jnp.float32) + 0.5

    def radius(j):
        return base + float(j)

    def own(j):
        r = radius(j)
        rate = STEP / r
        for h in (0, 32):
            rows = slice(h, h + 32)
            q = [u[f, 2 + j, rows] for f in range(FIELDS)]
            ur, ut, uz, p = primitives(q)
            e = q[4] + p
            cross = q[1] * ut
            swirl = q[2] * ut + p
            radial = [q[1], q[1] * ur + p, cross, q[3] * ur, e * ur]
            azimuth = [q[2], cross, swirl, q[3] * ut, e * ut]
            axial = [q[3], q[1] * uz, q[2] * uz, q[3] * uz + p, e * uz]
            grown = [q[0], q[1] + rate * swirl, q[2] - rate * cross, q[3], q[4]]
            for f in range(FIELDS):
                rf[f, 2 + j, rows] = r * radial[f]
                gs[f, j, 16 + h : 48 + h] = azimuth[f]
                sb[f, j, rows] = grown[f]
                high, low = split(axial[f])
                hh[j, 64 * f + h : 64 * f + h + 32, 0:128] = high
                hh[j, 64 * f + h : 64 * f + h + 32, 128:256] = low
        zd[j] = product(hh[j], dz[...])

    def far_flux(c):
        r = base + float(c - 2)
        for h in (0, 32):
            rows = slice(h, h + 32)
            q = [u[f, c, rows] for f in range(FIELDS)]
            ur, _, _, p = primitives(q)
            radial = [q[1], q[1] * ur + p, q[2] * ur, q[3] * ur, (q[4] + p) * ur]
            for f in range(FIELDS):
                rf[f, c, rows] = r * radial[f]

    turn = STEP / (12.0 * 2.0 * math.pi / (64 * sectors))

    def slope_angle(f, j, start, count):
        def part(offset):
            return gs[f, j, start + 16 + offset : start + 16 + offset + count]

        return (part(-2) - part(2)) + 8.0 * (part(1) - part(-1))

    def advance(j):
        kr = (STEP / 12.0) / radius(j)
        kt = turn / radius(j)
        for f in range(FIELDS):
            for h in (0, 32):
                rows = slice(h, h + 32)
                rad = (rf[f, j, rows] - rf[f, j + 4, rows]) + 8.0 * (rf[f, j + 3, rows] - rf[f, j + 1, rows])
                sg[f, j, rows] = (
                    sb[f, j, rows] - kr * rad - kt * slope_angle(f, j, h, 32) - (STEP / 12.0) * zd[j, 64 * f + h : 64 * f + h + 32]
                )

    def edges(j):
        kt = turn / radius(j)
        for f in range(FIELDS):
            sg[f, j, 64:72] = -kt * (slope_angle(f, j, 64, 8) + slope_angle(f, j, -8, 8))

    def pack(j):
        lane = lax.broadcasted_iota(jnp.int32, (8, 128), 1)
        row = lax.broadcasted_iota(jnp.int32, (8, 128), 0)
        edge = sg[4, j, 64:72]
        section = exchanged([sg[4, j, 16 * g : 16 * g + 16] for g in range(4)])
        mirror = exchanged([sg[4, j, 72 + 16 * g : 88 + 16 * g] for g in range(4)]) if j < 2 else []
        for q in range(4):
            pk[j, q, 0:16] = section[q]
            start = pltpu.roll(edge, (-32 * q) % 128, 1) if q else edge
            end = pltpu.roll(edge, 32 * (3 - q), 1) if q < 3 else edge
            pk[j, q, 16:24] = jnp.where(
                (row < 4) & (lane < 32), start, jnp.where((row >= 4) & (lane >= 96), end, 0.0)
            )
            if mirror:
                pk[j, q, 24:40] = mirror[q]

    def shifted(dx, dy):
        return lax.rem(y + dy, 4) * 4 + lax.rem(x + dx, 4)

    def forward(target, slot, rows):
        f, j, _ = units_of(target)
        return remote(sg.at[f, j, 0:rows], rx.at[az, 0:rows], fs.at[0, slot], fr.at[0, az], 0, target)

    def forward_quarter(target, slot, rows):
        q, _, j = units_of(target)
        return remote(pk.at[j, q, 0:rows], rq.at[az, 0:rows], fs.at[1, slot], fr.at[1, az], 0, target)

    def forward_all(inner, act):
        for i, (dx, dy) in enumerate(OFFSETS):
            target = shifted(dx, dy)
            whole = units_of(target)[1] < 2 if inner else units_of(target)[1] >= 2

            @pl.when(whole)
            def _():
                act(forward(target, i, 136 if inner else 72))

            @pl.when(jnp.logical_not(whole))
            def _():
                act(forward_quarter(target, i, 40 if inner else 24))

    my_f, my_j, my_quarter = units_of(az)
    my_inner = my_j < 2

    @pl.when(first)
    def _():
        for c in (4, 5):
            far_flux(c)
        for j in range(2):
            own(j)
        for j in range(2):
            advance(j)
            edges(j)
            kr = (STEP / 12.0) / radius(j)
            for f in range(FIELDS):
                inner = rf[f, 3] - 8.0 * rf[f, 2] if j == 0 else rf[f, 2]
                sg[f, j, 72:136] = (-SIGN[f] * kr) * inner
            pack(j)
        pl.semaphore_wait(barrier, sectors)
        forward_all(True, lambda c: c.start())
        up.start()
        for j in range(2, 4):
            own(j)

    @pl.when(blk > 0)
    def _():
        for j in range(4):
            own(j)
        ahead.wait_recv()
        behind.wait_recv()
        for side in range(2):
            for a in range(2):
                q = [halo[side, f, a] for f in range(FIELDS)]
                _, ut, _, p = primitives(q)
                azimuth = [q[2], q[1] * ut, q[2] * ut + p, q[3] * ut, (q[4] + p) * ut]
                row = (14 if side == 0 else 80) + a
                for f in range(FIELDS):
                    for j in range(4):
                        gs[f, j, row : row + 1] = azimuth[f][j : j + 1]
        up.wait_recv()
        for c in range(2):
            far_flux(c)

    @pl.when(last)
    def _():
        for f in range(FIELDS):
            for c in (6, 7):
                u[f, c] = u[f, 5]

    @pl.when(blk < blocks - 1)
    def _():
        down.wait_recv()

    for c in (6, 7):
        far_flux(c)

    def plain(j):
        return pltpu.make_async_copy(sg.at[:, j, 0:64], out.at[:, j], out_sem.at[j])

    @pl.when(first)
    def _():
        for j in range(2, 4):
            advance(j)
            edges(j)
            pack(j)
        forward_all(False, lambda c: c.start())

    @pl.when(blk > 0)
    def _():
        for j in range(4):
            advance(j)
            plain(j).start()

    def back(dx, dy):
        target = shifted(dx, dy)
        return remote(kp.at[target], out.at[my_f, my_j], bs.at[0, 4 * dy + dx], br.at[0, az], 0, target)

    def back_quarter(dx, dy):
        target = shifted(dx, dy)
        return remote(kq.at[target], qin.at[my_quarter, my_f], bs.at[1, 4 * dy + dx], br.at[1, az], 0, target)

    @pl.when(first)
    def _():
        for whole_inner in (True, False):
            rows, few = (136, 24) if whole_inner else (72, 40)

            @pl.when(my_inner if whole_inner else jnp.logical_not(my_inner))
            def _(rows=rows, few=few):
                mine = [
                    pltpu.make_async_copy(sg.at[my_f, my_j, 0:rows], rx.at[az, 0:rows], own_sem.at[0]),
                    pltpu.make_async_copy(pk.at[my_quarter, my_f, 0:few], rq.at[az, 0:few], own_sem.at[1]),
                ]
                for copy in mine:
                    copy.start()
                for copy in mine:
                    copy.wait()
                for i in others:
                    s = at(i)
                    remote(sg.at[0, 0, 0:rows], rx.at[s, 0:rows], fs.at[0, 0], fr.at[0, s], 0, s).wait_recv()
                    remote(pk.at[0, 0, 0:few], rq.at[s, 0:few], fs.at[1, 0], fr.at[1, s], 0, s).wait_recv()

                early = lax.broadcasted_iota(jnp.int32, (8, 128), 0) < 4
                group = lax.broadcasted_iota(jnp.int32, (16, 128), 1) // 32

                def gather(s, carry):
                    before = lax.rem(s + sectors - 1, sectors)
                    after = lax.rem(s + 1, sectors)
                    across = lax.rem(s + sectors // 2, sectors)
                    rx[s, 0:8] = rx[s, 0:8] + jnp.where(early, rx[before, 64:72], 0.0)
                    rx[s, 56:64] = rx[s, 56:64] + jnp.where(early, 0.0, rx[after, 64:72])
                    rq[s, 0:8] = rq[s, 0:8] + jnp.where(early, rq[before, 16:24], 0.0)
                    rq[s, 8:16] = rq[s, 8:16] + jnp.where(early, 0.0, rq[after, 16:24])
                    quarter = rq[s, 0:16]
                    if few == 40:
                        quarter = quarter + rq[across, 24:40]
                    for g in range(4):
                        value = rx[s, 16 * g : 16 * g + 16]
                        if rows == 136:
                            value = value + rx[across, 72 + 16 * g : 88 + 16 * g]
                        to = pl.ds(pl.multiple_of(256 * g + s * 16, 16), 16)
                        high, low = split(value)
                        xs[to, 0:128] = high
                        xs[to, 128:256] = low
                        high, low = split(jnp.where(group == g, quarter, 0.0))
                        xs[to, 256:384] = high
                        xs[to, 384:512] = low
                    return carry

                lax.fori_loop(0, sectors, gather, 0)

        fetch.wait()
        order = lax.rem(lax.broadcasted_iota(jnp.int32, (2 * MMAX, 128), 0), MMAX)
        scale = jnp.where(order == 0, 1.0, 2.0) / float(64 * sectors)
        sides = []
        for n, cycle in ((0, my_j), (256, my_quarter)):
            parts = product(tt[0, 0:256], xs[0:256, n : n + 256])
            for k in range(256, 64 * sectors, 256):
                parts = parts + product(tt[0, k : k + 256], xs[k : k + 256, n : n + 256])
            parts = parts[0:128] + parts[128:256]
            coef = parts[:, 0:128] + parts[:, 128:256]
            if n:
                coef = coef + pltpu.roll(coef, 64, 1)
                coef = coef + pltpu.roll(coef, 32, 1)
            sides.extend(split(coef * jnp.where(order < cut[cycle], scale, 0.0)))
        both = jnp.concatenate(sides, 1)
        both = jnp.concatenate([both, both], 0)
        group = lax.broadcasted_iota(jnp.int32, (16, 128), 1) // 32
        for dy in (2, 1, 3, 0):
            yy = lax.rem(y + dy, 4)
            kept = product(tt[1, pl.ds(pl.multiple_of(yy * 256, 256), 256)], both)
            whole = kept[:, 0:128] + kept[:, 128:256]
            part = kept[:, 256:384] + kept[:, 384:512]
            for i in range(4):
                kp[yy * 4 + i] = whole[64 * i : 64 * i + 64]
                packed = part[64 * i : 64 * i + 16]
                for g in range(1, 4):
                    packed = jnp.where(group == g, part[64 * i + 16 * g : 64 * i + 16 * g + 16], packed)
                kq[yy * 4 + i] = packed
            for dx in (2, 1, 3, 0):
                if dx or dy:
                    back_quarter(dx, dy).start()
                    back(dx, dy).start()
        mine = [
            pltpu.make_async_copy(kp.at[az], out.at[my_f, my_j], own_sem.at[0]),
            pltpu.make_async_copy(kq.at[az], qin.at[my_quarter, my_f], own_sem.at[1]),
        ]
        for copy in mine:
            copy.start()
        for copy in mine:
            copy.wait()
        for i in others:
            o = at(i)
            q, _, j = units_of(o)
            remote(kq.at[0], qin.at[j, q], bs.at[1, 0], br.at[1, o], 0, o).wait_recv()
        for j in range(4):
            for g, value in enumerate(exchanged([qin[j, q] for q in range(4)])):
                o4[j, 16 * g : 16 * g + 16] = value
        last_field = pltpu.make_async_copy(o4, out.at[4], own_sem.at[0])
        last_field.start()
        for i in others:
            o = at(i)
            f, j, _ = units_of(o)
            remote(kp.at[0], out.at[f, j], bs.at[0, 0], br.at[0, o], 0, o).wait_recv()
        last_field.wait()
        up.wait_send()
        forward_all(True, lambda c: c.wait_send())
        forward_all(False, lambda c: c.wait_send())
        for dx, dy in OFFSETS:
            back(dx, dy).wait_send()
            back_quarter(dx, dy).wait_send()

    @pl.when(blk > 0)
    def _():
        for j in range(4):
            plain(j).wait()
        down.wait_send()

        @pl.when(blk < blocks - 1)
        def _():
            up.wait_send()

        ahead.wait_send()
        behind.wait_send()


def place(held, out, sems):
    copies = [pltpu.make_async_copy(held.at[:, j], out.at[:, :, j], sems.at[j]) for j in range(4)]
    for copy in copies:
        copy.start()
    for copy in copies:
        copy.wait()


def shards(cut_table, blocks, sectors, state, cutoffs):
    points = state.shape[3]
    f32, bf16 = jnp.float32, jnp.bfloat16
    dma = pltpu.SemaphoreType.DMA
    anywhere = pl.BlockSpec(memory_space=pl.ANY)
    total = 64 * sectors
    held = pl.pallas_call(
        functools.partial(kernel, blocks, sectors),
        out_shape=jax.ShapeDtypeStruct((FIELDS, 4, 64, points), f32),
        in_specs=[pl.BlockSpec(memory_space=pltpu.SMEM)] + [anywhere] * 2,
        out_specs=anywhere,
        scratch_shapes=[
            pltpu.VMEM((FIELDS, 8, 64, points), f32),
            pltpu.VMEM((FIELDS, 8, 64, points), f32),
            pltpu.VMEM((FIELDS, 4, 96, points), f32),
            pltpu.VMEM((4, FIELDS * 64, 2 * points), bf16),
            pltpu.VMEM((4, FIELDS * 64, points), f32),
            pltpu.VMEM((FIELDS, 4, 64, points), f32),
            pltpu.VMEM((FIELDS, 4, 136, points), f32),
            pltpu.VMEM((2, FIELDS, 2, 4, points), f32),
            pltpu.VMEM((sectors, 136, points), f32),
            pltpu.VMEM((sectors, 40, points), f32),
            pltpu.VMEM((4, 4, 40, points), f32),
            pltpu.VMEM((total, 4 * points), bf16),
            pltpu.VMEM((sectors, 64, points), f32),
            pltpu.VMEM((sectors, 16, points), f32),
            pltpu.VMEM((4, 4, 16, points), f32),
            pltpu.VMEM((4, 64, points), f32),
            pltpu.VMEM((2, total, 4 * MMAX), bf16),
            pltpu.VMEM((2 * points, points), bf16),
            dma((4,)),
            dma((1,)),
            dma((4,)),
            dma((4,)),
            dma((2, sectors)),
            dma((2, sectors)),
            dma((2, sectors)),
            dma((2, sectors)),
            dma((2,)),
            dma((4,)),
        ],
        compiler_params=pltpu.CompilerParams(
            collective_id=0, has_side_effects=True, vmem_limit_bytes=LIMIT_MIB * 1024 * 1024
        ),
        name="section",
    )(cutoffs, state, jnp.asarray(cut_table))
    return pl.pallas_call(
        place,
        out_shape=jax.ShapeDtypeStruct(state.shape, f32),
        in_specs=[anywhere],
        out_specs=anywhere,
        scratch_shapes=[dma((4,))],
        compiler_params=pltpu.CompilerParams(vmem_limit_bytes=1024 * 1024),
        name="place",
    )(held)


def solution(mesh):
    blocks, sectors = mesh.shape["blk"], mesh.shape["az"]
    placed = (P(None, "az", "blk", None), P())
    return jax.shard_map(
        functools.partial(shards, tables(64 * sectors), blocks, sectors),
        mesh=mesh,
        in_specs=placed,
        out_specs=P(None, "az", "blk", None),
        check_vma=False,
    )
```

```python
import functools
import math

import jax
import jax.numpy as jnp
import ml_dtypes
import numpy as np
from jax import lax
from jax.experimental import pallas as pl
from jax.experimental.pallas import tpu as pltpu
from jax.sharding import PartitionSpec as P

MESH = pl.DeviceIdType.MESH
FIELDS = 5
MMAX = 64
GAS = 0.4
STEP = 0.025
SIGN = (1.0, -1.0, -1.0, 1.0, 1.0)
LIMIT_MIB = 53


OFFSETS = sorted(
    ((dx, dy) for dx in range(4) for dy in range(4) if dx or dy),
    key=lambda o: -(min(o[0], 4 - o[0]) + min(o[1], 4 - o[1])),
)


def tables(total):
    product = (np.arange(MMAX)[:, None] * np.arange(total)[None, :]) % total
    angle = product * (2.0 * math.pi / total)
    both = np.concatenate([np.cos(angle), np.sin(angle)], 0)
    high = both.astype(ml_dtypes.bfloat16)
    low = (both - high.astype(np.float64)).astype(ml_dtypes.bfloat16)
    parts = np.concatenate([high, low], 0)
    blocked = parts.reshape(4 * MMAX, total // 64, 4, 16).transpose(2, 0, 1, 3).reshape(total, 256)
    return np.stack([blocked, parts.T])


def units_of(az):
    t = lax.rem(az + az // 4, 4)
    odd, upper = lax.rem(t, 2), t // 2
    return az // 4, 2 * odd + upper, 2 * (1 - odd) + upper


def exchanged(pieces):
    group = lax.broadcasted_iota(jnp.int32, pieces[0].shape, 1) // 32
    out = []
    for a in range(4):
        value = pieces[a]
        for b in range(4):
            if b != a:
                value = jnp.where(group == b, pltpu.roll(pieces[b], (32 * (b - a)) % 128, 1), value)
        out.append(value)
    return out


def split(value):
    high = value.astype(jnp.bfloat16)
    return high, (value - high.astype(jnp.float32)).astype(jnp.bfloat16)


def product(a, b):
    return jnp.dot(a, b, preferred_element_type=jnp.float32)


def axial_matrix():
    point = lax.rem(lax.broadcasted_iota(jnp.int32, (256, 128), 0), 128)
    at = lax.broadcasted_iota(jnp.int32, (256, 128), 1)
    total = jnp.zeros((256, 128), jnp.float32)
    for offset, c in ((-2, 1.0), (-1, -8.0), (1, 8.0), (2, -1.0)):
        total = total + jnp.where(point == jnp.clip(at + offset, 0, 127), c, 0.0)
    return total.astype(jnp.bfloat16)


def primitives(q):
    inv = 1.0 / q[0]
    ur, ut, uz = q[1] * inv, q[2] * inv, q[3] * inv
    p = GAS * (q[4] - 0.5 * (q[1] * ur + q[2] * ut + q[3] * uz))
    return ur, ut, uz, p


def kernel(blocks, sectors, cut, state, transforms, out, u, rf, gs, hh, zd, sb, sg, halo,
           rx, rq, pk, xs, kp, kq, qin, o4, tt, dz, load_sem, table_sem, hs, hr, fs, fr, bs, br, own_sem, out_sem):
    blk = lax.axis_index("blk")
    az = lax.axis_index("az")
    first = blk == 0
    last = blk == blocks - 1
    x, y = lax.rem(az, 4), az // 4
    apart = az == 0
    owner = (first & jnp.logical_not(apart)) | ((blk == 1) & apart)
    others = range(1, sectors)

    def at(i):
        return lax.rem(az + i, sectors)

    loads = [pltpu.make_async_copy(state.at[:, :, j], u.at[:, 2 + j], load_sem.at[j]) for j in range(4)]
    for copy in loads:
        copy.start()
    fetch = pltpu.make_async_copy(transforms, tt, table_sem.at[0])

    barrier = pltpu.get_barrier_semaphore()

    def greet(b, a):
        pl.semaphore_signal(barrier, inc=1, device_id=(b, a), device_id_type=MESH)

    @pl.when(first)
    def _():
        greet(1, az)

        @pl.when(jnp.logical_not(apart))
        def _():
            for i in others:
                greet(0, at(i))

    @pl.when((blk == 1) & apart)
    def _():
        for i in others:
            greet(0, at(i))

    @pl.when(owner)
    def _():
        fetch.start()

    @pl.when(blk > 0)
    def _():
        greet(blk - 1, az)
        greet(blk, at(1))
        greet(blk, at(sectors - 1))

        @pl.when(blk < blocks - 1)
        def _():
            greet(blk + 1, az)

    def remote(src, dst, send, recv, b, a):
        return pltpu.make_async_remote_copy(
            src_ref=src, dst_ref=dst, send_sem=send, recv_sem=recv, device_id=(b, a), device_id_type=MESH
        )

    up = remote(u.at[:, 4:6], u.at[:, 0:2], hs.at[0], hr.at[0], jnp.minimum(blk + 1, blocks - 1), az)
    down = remote(u.at[:, 2:4], u.at[:, 6:8], hs.at[1], hr.at[1], jnp.maximum(blk - 1, 0), az)
    ahead = remote(state.at[:, 62:64], halo.at[0], hs.at[2], hr.at[2], blk, at(1))
    behind = remote(state.at[:, 0:2], halo.at[1], hs.at[3], hr.at[3], blk, at(sectors - 1))

    dz[...] = axial_matrix()

    @pl.when(first)
    def _():
        zero = jnp.zeros((64, 128), jnp.float32)
        for f in range(FIELDS):
            for c in range(2):
                rf[f, c] = zero
            for j in range(4):
                gs[f, j, 0:16] = zero[:16]
                gs[f, j, 80:96] = zero[:16]

    for copy in loads:
        copy.wait()

    @pl.when(blk > 0)
    def _():
        @pl.when(blk < blocks - 1)
        def _():
            pl.semaphore_wait(barrier, 4)

        @pl.when(last)
        def _():
            pl.semaphore_wait(barrier, 3)

        down.start()

        @pl.when(blk < blocks - 1)
        def _():
            up.start()

        ahead.start()
        behind.start()

    base = (blk * 4).astype(jnp.float32) + 0.5

    def radius(j):
        return base + float(j)

    def own(j):
        r = radius(j)
        rate = STEP / r
        for h in (0, 32):
            rows = slice(h, h + 32)
            q = [u[f, 2 + j, rows] for f in range(FIELDS)]
            ur, ut, uz, p = primitives(q)
            e = q[4] + p
            cross = q[1] * ut
            swirl = q[2] * ut + p
            radial = [q[1], q[1] * ur + p, cross, q[3] * ur, e * ur]
            azimuth = [q[2], cross, swirl, q[3] * ut, e * ut]
            axial = [q[3], q[1] * uz, q[2] * uz, q[3] * uz + p, e * uz]
            grown = [q[0], q[1] + rate * swirl, q[2] - rate * cross, q[3], q[4]]
            for f in range(FIELDS):
                rf[f, 2 + j, rows] = r * radial[f]
                gs[f, j, 16 + h : 48 + h] = azimuth[f]
                sb[f, j, rows] = grown[f]
                high, low = split(axial[f])
                hh[j, 64 * f + h : 64 * f + h + 32, 0:128] = high
                hh[j, 64 * f + h : 64 * f + h + 32, 128:256] = low
        zd[j] = product(hh[j], dz[...])

    def far_flux(c):
        r = base + float(c - 2)
        for h in (0, 32):
            rows = slice(h, h + 32)
            q = [u[f, c, rows] for f in range(FIELDS)]
            ur, _, _, p = primitives(q)
            radial = [q[1], q[1] * ur + p, q[2] * ur, q[3] * ur, (q[4] + p) * ur]
            for f in range(FIELDS):
                rf[f, c, rows] = r * radial[f]

    turn = STEP / (12.0 * 2.0 * math.pi / (64 * sectors))

    def slope_angle(f, j, start, count):
        def part(offset):
            return gs[f, j, start + 16 + offset : start + 16 + offset + count]

        return (part(-2) - part(2)) + 8.0 * (part(1) - part(-1))

    def advance(j):
        kr = (STEP / 12.0) / radius(j)
        kt = turn / radius(j)
        for f in range(FIELDS):
            for h in (0, 32):
                rows = slice(h, h + 32)
                rad = (rf[f, j, rows] - rf[f, j + 4, rows]) + 8.0 * (rf[f, j + 3, rows] - rf[f, j + 1, rows])
                sg[f, j, rows] = (
                    sb[f, j, rows] - kr * rad - kt * slope_angle(f, j, h, 32) - (STEP / 12.0) * zd[j, 64 * f + h : 64 * f + h + 32]
                )

    def edges(j):
        kt = turn / radius(j)
        for f in range(FIELDS):
            sg[f, j, 64:72] = -kt * (slope_angle(f, j, 64, 8) + slope_angle(f, j, -8, 8))

    def pack(j):
        lane = lax.broadcasted_iota(jnp.int32, (8, 128), 1)
        row = lax.broadcasted_iota(jnp.int32, (8, 128), 0)
        edge = sg[4, j, 64:72]
        section = exchanged([sg[4, j, 16 * g : 16 * g + 16] for g in range(4)])
        mirror = exchanged([sg[4, j, 72 + 16 * g : 88 + 16 * g] for g in range(4)]) if j < 2 else []
        for q in range(4):
            pk[j, q, 0:16] = section[q]
            start = pltpu.roll(edge, (-32 * q) % 128, 1) if q else edge
            end = pltpu.roll(edge, 32 * (3 - q), 1) if q < 3 else edge
            pk[j, q, 16:24] = jnp.where(
                (row < 4) & (lane < 32), start, jnp.where((row >= 4) & (lane >= 96), end, 0.0)
            )
            if mirror:
                pk[j, q, 24:40] = mirror[q]

    def shifted(dx, dy):
        return lax.rem(y + dy, 4) * 4 + lax.rem(x + dx, 4)

    def home(target):
        return jnp.where(target == 0, 1, 0)

    def forward(target, slot, rows):
        f, j, _ = units_of(target)
        return remote(sg.at[f, j, 0:rows], rx.at[az, 0:rows], fs.at[0, slot], fr.at[0, az], home(target), target)

    def forward_quarter(target, slot, rows):
        q, _, j = units_of(target)
        return remote(pk.at[j, q, 0:rows], rq.at[az, 0:rows], fs.at[1, slot], fr.at[1, az], home(target), target)

    def forward_all(inner, act):
        for i, (dx, dy) in enumerate(OFFSETS + [(0, 0)]):
            target = shifted(dx, dy)
            whole = units_of(target)[1] < 2 if inner else units_of(target)[1] >= 2
            away = True if dx or dy else apart

            @pl.when(whole & away)
            def _():
                act(forward(target, i, 136 if inner else 72))

            @pl.when(jnp.logical_not(whole) & away)
            def _():
                act(forward_quarter(target, i, 40 if inner else 24))

    my_f, my_j, my_quarter = units_of(az)
    my_inner = my_j < 2

    @pl.when(first)
    def _():
        for c in (4, 5):
            far_flux(c)
        for j in range(2):
            own(j)
        for j in range(2):
            advance(j)
            edges(j)
            kr = (STEP / 12.0) / radius(j)
            for f in range(FIELDS):
                inner = rf[f, 3] - 8.0 * rf[f, 2] if j == 0 else rf[f, 2]
                sg[f, j, 72:136] = (-SIGN[f] * kr) * inner
            pack(j)
        pl.semaphore_wait(barrier, sectors)
        forward_all(True, lambda c: c.start())
        up.start()
        for j in range(2, 4):
            own(j)

    @pl.when(blk > 0)
    def _():
        for j in range(4):
            own(j)
        ahead.wait_recv()
        behind.wait_recv()
        for side in range(2):
            for a in range(2):
                q = [halo[side, f, a] for f in range(FIELDS)]
                _, ut, _, p = primitives(q)
                azimuth = [q[2], q[1] * ut, q[2] * ut + p, q[3] * ut, (q[4] + p) * ut]
                row = (14 if side == 0 else 80) + a
                for f in range(FIELDS):
                    for j in range(4):
                        gs[f, j, row : row + 1] = azimuth[f][j : j + 1]
        up.wait_recv()
        for c in range(2):
            far_flux(c)

    @pl.when(last)
    def _():
        for f in range(FIELDS):
            for c in (6, 7):
                u[f, c] = u[f, 5]

    @pl.when(blk < blocks - 1)
    def _():
        down.wait_recv()

    for c in (6, 7):
        far_flux(c)

    def plain(j):
        return pltpu.make_async_copy(sg.at[:, j, 0:64], out.at[:, j], out_sem.at[j])

    @pl.when(first)
    def _():
        for j in range(2, 4):
            advance(j)
            edges(j)
            pack(j)
        forward_all(False, lambda c: c.start())

    @pl.when(blk > 0)
    def _():
        for j in range(4):
            advance(j)
            plain(j).start()

    def back(dx, dy):
        target = shifted(dx, dy)
        return remote(kp.at[target], out.at[my_f, my_j], bs.at[0, 4 * dy + dx], br.at[0, az], 0, target)

    def back_quarter(dx, dy):
        target = shifted(dx, dy)
        return remote(kq.at[target], qin.at[my_quarter, my_f], bs.at[1, 4 * dy + dx], br.at[1, az], 0, target)

    @pl.when(owner)
    def _():
        for whole_inner in (True, False):
            rows, few = (136, 24) if whole_inner else (72, 40)

            @pl.when(my_inner if whole_inner else jnp.logical_not(my_inner))
            def _(rows=rows, few=few):
                mine = [
                    pltpu.make_async_copy(sg.at[my_f, my_j, 0:rows], rx.at[az, 0:rows], own_sem.at[0]),
                    pltpu.make_async_copy(pk.at[my_quarter, my_f, 0:few], rq.at[az, 0:few], own_sem.at[1]),
                ]

                def arrived(s):
                    remote(sg.at[0, 0, 0:rows], rx.at[s, 0:rows], fs.at[0, 0], fr.at[0, s], 0, s).wait_recv()
                    remote(pk.at[0, 0, 0:few], rq.at[s, 0:few], fs.at[1, 0], fr.at[1, s], 0, s).wait_recv()

                @pl.when(first)
                def _():
                    for copy in mine:
                        copy.start()
                    for copy in mine:
                        copy.wait()

                @pl.when(blk > 0)
                def _():
                    arrived(az)

                for i in others:
                    arrived(at(i))

                early = lax.broadcasted_iota(jnp.int32, (8, 128), 0) < 4
                group = lax.broadcasted_iota(jnp.int32, (16, 128), 1) // 32

                def gather(s, carry):
                    before = lax.rem(s + sectors - 1, sectors)
                    after = lax.rem(s + 1, sectors)
                    across = lax.rem(s + sectors // 2, sectors)
                    rx[s, 0:8] = rx[s, 0:8] + jnp.where(early, rx[before, 64:72], 0.0)
                    rx[s, 56:64] = rx[s, 56:64] + jnp.where(early, 0.0, rx[after, 64:72])
                    rq[s, 0:8] = rq[s, 0:8] + jnp.where(early, rq[before, 16:24], 0.0)
                    rq[s, 8:16] = rq[s, 8:16] + jnp.where(early, 0.0, rq[after, 16:24])
                    quarter = rq[s, 0:16]
                    if few == 40:
                        quarter = quarter + rq[across, 24:40]
                    for g in range(4):
                        value = rx[s, 16 * g : 16 * g + 16]
                        if rows == 136:
                            value = value + rx[across, 72 + 16 * g : 88 + 16 * g]
                        to = pl.ds(pl.multiple_of(256 * g + s * 16, 16), 16)
                        high, low = split(value)
                        xs[to, 0:128] = high
                        xs[to, 128:256] = low
                        high, low = split(jnp.where(group == g, quarter, 0.0))
                        xs[to, 256:384] = high
                        xs[to, 384:512] = low
                    return carry

                lax.fori_loop(0, sectors, gather, 0)

        fetch.wait()
        order = lax.rem(lax.broadcasted_iota(jnp.int32, (2 * MMAX, 128), 0), MMAX)
        scale = jnp.where(order == 0, 1.0, 2.0) / float(64 * sectors)
        sides = []
        for n, cycle in ((0, my_j), (256, my_quarter)):
            parts = product(tt[0, 0:256], xs[0:256, n : n + 256])
            for k in range(256, 64 * sectors, 256):
                parts = parts + product(tt[0, k : k + 256], xs[k : k + 256, n : n + 256])
            parts = parts[0:128] + parts[128:256]
            coef = parts[:, 0:128] + parts[:, 128:256]
            if n:
                coef = coef + pltpu.roll(coef, 64, 1)
                coef = coef + pltpu.roll(coef, 32, 1)
            sides.extend(split(coef * jnp.where(order < cut[cycle], scale, 0.0)))
        both = jnp.concatenate(sides, 1)
        both = jnp.concatenate([both, both], 0)
        group = lax.broadcasted_iota(jnp.int32, (16, 128), 1) // 32
        for dy in (2, 1, 3, 0):
            yy = lax.rem(y + dy, 4)
            kept = product(tt[1, pl.ds(pl.multiple_of(yy * 256, 256), 256)], both)
            whole = kept[:, 0:128] + kept[:, 128:256]
            part = kept[:, 256:384] + kept[:, 384:512]
            for i in range(4):
                kp[yy * 4 + i] = whole[64 * i : 64 * i + 64]
                packed = part[64 * i : 64 * i + 16]
                for g in range(1, 4):
                    packed = jnp.where(group == g, part[64 * i + 16 * g : 64 * i + 16 * g + 16], packed)
                kq[yy * 4 + i] = packed
            for dx in (2, 1, 3, 0):
                if dx or dy:
                    back_quarter(dx, dy).start()
                    back(dx, dy).start()

        @pl.when(blk > 0)
        def _():
            back_quarter(0, 0).start()
            back(0, 0).start()

        @pl.when(first)
        def _():
            mine = [
                pltpu.make_async_copy(kp.at[az], out.at[my_f, my_j], own_sem.at[0]),
                pltpu.make_async_copy(kq.at[az], qin.at[my_quarter, my_f], own_sem.at[1]),
            ]
            for copy in mine:
                copy.start()
            for copy in mine:
                copy.wait()

    @pl.when(first)
    def _():
        def quarter_back(o):
            q, _, j = units_of(o)
            remote(kq.at[0], qin.at[j, q], bs.at[1, 0], br.at[1, o], home(o), o).wait_recv()

        def whole_back(o):
            f, j, _ = units_of(o)
            remote(kp.at[0], out.at[f, j], bs.at[0, 0], br.at[0, o], home(o), o).wait_recv()

        for i in others:
            quarter_back(at(i))

        @pl.when(apart)
        def _():
            quarter_back(az)
            whole_back(az)

        for j in range(4):
            for g, value in enumerate(exchanged([qin[j, q] for q in range(4)])):
                o4[j, 16 * g : 16 * g + 16] = value
        last_field = pltpu.make_async_copy(o4, out.at[4], own_sem.at[0])
        last_field.start()
        for i in others:
            whole_back(at(i))
        last_field.wait()
        up.wait_send()
        forward_all(True, lambda c: c.wait_send())
        forward_all(False, lambda c: c.wait_send())

    @pl.when(owner)
    def _():
        for dx, dy in OFFSETS:
            back(dx, dy).wait_send()
            back_quarter(dx, dy).wait_send()

        @pl.when(blk > 0)
        def _():
            back(0, 0).wait_send()
            back_quarter(0, 0).wait_send()

    @pl.when(blk > 0)
    def _():
        for j in range(4):
            plain(j).wait()
        down.wait_send()

        @pl.when(blk < blocks - 1)
        def _():
            up.wait_send()

        ahead.wait_send()
        behind.wait_send()


def place(held, out, sems):
    copies = [pltpu.make_async_copy(held.at[:, j], out.at[:, :, j], sems.at[j]) for j in range(4)]
    for copy in copies:
        copy.start()
    for copy in copies:
        copy.wait()


def shards(cut_table, blocks, sectors, state, cutoffs):
    points = state.shape[3]
    f32, bf16 = jnp.float32, jnp.bfloat16
    dma = pltpu.SemaphoreType.DMA
    anywhere = pl.BlockSpec(memory_space=pl.ANY)
    total = 64 * sectors
    held = pl.pallas_call(
        functools.partial(kernel, blocks, sectors),
        out_shape=jax.ShapeDtypeStruct((FIELDS, 4, 64, points), f32),
        in_specs=[pl.BlockSpec(memory_space=pltpu.SMEM)] + [anywhere] * 2,
        out_specs=anywhere,
        scratch_shapes=[
            pltpu.VMEM((FIELDS, 8, 64, points), f32),
            pltpu.VMEM((FIELDS, 8, 64, points), f32),
            pltpu.VMEM((FIELDS, 4, 96, points), f32),
            pltpu.VMEM((4, FIELDS * 64, 2 * points), bf16),
            pltpu.VMEM((4, FIELDS * 64, points), f32),
            pltpu.VMEM((FIELDS, 4, 64, points), f32),
            pltpu.VMEM((FIELDS, 4, 136, points), f32),
            pltpu.VMEM((2, FIELDS, 2, 4, points), f32),
            pltpu.VMEM((sectors, 136, points), f32),
            pltpu.VMEM((sectors, 40, points), f32),
            pltpu.VMEM((4, 4, 40, points), f32),
            pltpu.VMEM((total, 4 * points), bf16),
            pltpu.VMEM((sectors, 64, points), f32),
            pltpu.VMEM((sectors, 16, points), f32),
            pltpu.VMEM((4, 4, 16, points), f32),
            pltpu.VMEM((4, 64, points), f32),
            pltpu.VMEM((2, total, 4 * MMAX), bf16),
            pltpu.VMEM((2 * points, points), bf16),
            dma((4,)),
            dma((1,)),
            dma((4,)),
            dma((4,)),
            dma((2, sectors)),
            dma((2, sectors)),
            dma((2, sectors)),
            dma((2, sectors)),
            dma((2,)),
            dma((4,)),
        ],
        compiler_params=pltpu.CompilerParams(
            collective_id=0, has_side_effects=True, vmem_limit_bytes=LIMIT_MIB * 1024 * 1024
        ),
        name="section",
    )(cutoffs, state, jnp.asarray(cut_table))
    return pl.pallas_call(
        place,
        out_shape=jax.ShapeDtypeStruct(state.shape, f32),
        in_specs=[anywhere],
        out_specs=anywhere,
        scratch_shapes=[dma((4,))],
        compiler_params=pltpu.CompilerParams(vmem_limit_bytes=1024 * 1024),
        name="place",
    )(held)


def solution(mesh):
    blocks, sectors = mesh.shape["blk"], mesh.shape["az"]
    placed = (P(None, "az", "blk", None), P())
    return jax.shard_map(
        functools.partial(shards, tables(64 * sectors), blocks, sectors),
        mesh=mesh,
        in_specs=placed,
        out_specs=P(None, "az", "blk", None),
        check_vma=False,
    )
```

```python
import functools
import math

import jax
import jax.numpy as jnp
import ml_dtypes
import numpy as np
from jax import lax
from jax.experimental import pallas as pl
from jax.experimental.pallas import tpu as pltpu
from jax.sharding import PartitionSpec as P

MESH = pl.DeviceIdType.MESH
FIELDS = 5
MMAX = 64
RANK = 32
GAS = 0.4
STEP = 0.025
SIGN = (1.0, -1.0, -1.0, 1.0, 1.0)
LIMIT_MIB = 53


OFFSETS = sorted(
    ((dx, dy) for dx in range(4) for dy in range(4) if dx or dy),
    key=lambda o: -(min(o[0], 4 - o[0]) + min(o[1], 4 - o[1])),
)


def halves(values):
    high = values.astype(ml_dtypes.bfloat16)
    return high, (values - high.astype(np.float64)).astype(ml_dtypes.bfloat16)


def tables(total):
    window = np.arange(-2, 66)
    basis, _ = np.linalg.qr(np.polynomial.legendre.legvander((window - 31.5) / 33.5, RANK - 1))
    rows = np.zeros((80, RANK))
    rows[window % 72] = basis
    modes = np.arange(MMAX)[:, None]
    angle = modes * window[None, :] * (2.0 * math.pi / total)
    even, odd = np.cos(angle) @ basis, np.sin(angle) @ basis
    turn = (modes * 64 * np.arange(total // 64)[None, :]) % total * (2.0 * math.pi / total)
    cos_t, sin_t = np.cos(turn)[:, :, None], np.sin(turn)[:, :, None]
    even, odd = even[:, None, :], odd[:, None, :]
    both = np.concatenate([cos_t * even - sin_t * odd, sin_t * even + cos_t * odd], 0)
    both = both.reshape(2 * MMAX, -1)
    forth = np.concatenate(halves(both), 0)
    grouped = forth.reshape(4 * MMAX, -1, 4, 8).transpose(2, 0, 1, 3).reshape(16 * MMAX, -1)
    shrink = np.concatenate(halves(rows.T), 0)
    grow = np.concatenate(halves(rows[:64]), 1)
    out = np.zeros((4096, 128), ml_dtypes.bfloat16)
    out[0:1024] = grouped
    out[1024:1536], out[1536:2048] = forth.T[:, 0:128], forth.T[:, 128:256]
    out[2048:2112, 0:80], out[2112:2176, 0:64] = shrink, grow
    return out


def units_of(az):
    t = lax.rem(az + az // 4, 4)
    odd, upper = lax.rem(t, 2), t // 2
    return az // 4, 2 * odd + upper, 2 * (1 - odd) + upper


def exchanged(pieces):
    group = lax.broadcasted_iota(jnp.int32, pieces[0].shape, 1) // 32
    out = []
    for a in range(4):
        value = pieces[a]
        for b in range(4):
            if b != a:
                value = jnp.where(group == b, pltpu.roll(pieces[b], (32 * (b - a)) % 128, 1), value)
        out.append(value)
    return out


def split(value):
    high = value.astype(jnp.bfloat16)
    return high, (value - high.astype(jnp.float32)).astype(jnp.bfloat16)


def product(a, b):
    return jnp.dot(a, b, preferred_element_type=jnp.float32)


def axial_matrix():
    point = lax.rem(lax.broadcasted_iota(jnp.int32, (256, 128), 0), 128)
    at = lax.broadcasted_iota(jnp.int32, (256, 128), 1)
    total = jnp.zeros((256, 128), jnp.float32)
    for offset, c in ((-2, 1.0), (-1, -8.0), (1, 8.0), (2, -1.0)):
        total = total + jnp.where(point == jnp.clip(at + offset, 0, 127), c, 0.0)
    return total.astype(jnp.bfloat16)


def primitives(q):
    inv = 1.0 / q[0]
    ur, ut, uz = q[1] * inv, q[2] * inv, q[3] * inv
    p = GAS * (q[4] - 0.5 * (q[1] * ur + q[2] * ut + q[3] * uz))
    return ur, ut, uz, p


def kernel(blocks, sectors, cut, state, transforms, out, u, rf, gs, hh, zd, sb, sg, halo,
           yw, rx, rq, pk, xs, kp, kq, qin, zin, small, large, forth, home_again, dz, load_sem, table_sem, hs, hr, fs, fr, bs, br, own_sem, out_sem):
    blk = lax.axis_index("blk")
    az = lax.axis_index("az")
    first = blk == 0
    last = blk == blocks - 1
    x, y = lax.rem(az, 4), az // 4
    apart = az == 0
    owner = (first & jnp.logical_not(apart)) | ((blk == 1) & apart)
    others = range(1, sectors)

    def at(i):
        return lax.rem(az + i, sectors)

    loads = [pltpu.make_async_copy(state.at[:, :, j], u.at[:, 2 + j], load_sem.at[j]) for j in range(4)]
    for copy in loads:
        copy.start()
    fetch = [
        pltpu.make_async_copy(transforms.at[a:b], to, table_sem.at[n])
        for n, (a, b, to) in enumerate(
            (
                (2048, 2112, small),
                (2112, 2176, large),
                (0, 1024, forth),
                (1024, 1536, home_again.at[:, 0:128]),
                (1536, 2048, home_again.at[:, 128:256]),
            )
        )
    ]

    barrier = pltpu.get_barrier_semaphore()

    def greet(b, a):
        pl.semaphore_signal(barrier, inc=1, device_id=(b, a), device_id_type=MESH)

    @pl.when(first)
    def _():
        greet(1, az)

        @pl.when(jnp.logical_not(apart))
        def _():
            for i in others:
                greet(0, at(i))

    @pl.when((blk == 1) & apart)
    def _():
        for i in others:
            greet(0, at(i))

    @pl.when(first)
    def _():
        for copy in fetch[:2]:
            copy.start()

    @pl.when(owner)
    def _():
        for copy in fetch[2:]:
            copy.start()

    @pl.when(blk > 0)
    def _():
        greet(blk - 1, az)
        greet(blk, at(1))
        greet(blk, at(sectors - 1))

        @pl.when(blk < blocks - 1)
        def _():
            greet(blk + 1, az)

    def remote(src, dst, send, recv, b, a):
        return pltpu.make_async_remote_copy(
            src_ref=src, dst_ref=dst, send_sem=send, recv_sem=recv, device_id=(b, a), device_id_type=MESH
        )

    up = remote(u.at[:, 4:6], u.at[:, 0:2], hs.at[0], hr.at[0], jnp.minimum(blk + 1, blocks - 1), az)
    down = remote(u.at[:, 2:4], u.at[:, 6:8], hs.at[1], hr.at[1], jnp.maximum(blk - 1, 0), az)
    ahead = remote(state.at[:, 62:64], halo.at[0], hs.at[2], hr.at[2], blk, at(1))
    behind = remote(state.at[:, 0:2], halo.at[1], hs.at[3], hr.at[3], blk, at(sectors - 1))

    dz[...] = axial_matrix()

    @pl.when(first)
    def _():
        zero = jnp.zeros((64, 128), jnp.float32)
        for f in range(FIELDS):
            for c in range(2):
                rf[f, c] = zero
            for j in range(4):
                gs[f, j, 0:16] = zero[:16]
                gs[f, j, 80:96] = zero[:16]
                sg[f, j, 72:80] = zero[:8]

    for copy in loads:
        copy.wait()

    @pl.when(blk > 0)
    def _():
        @pl.when(blk < blocks - 1)
        def _():
            pl.semaphore_wait(barrier, 4)

        @pl.when(last)
        def _():
            pl.semaphore_wait(barrier, 3)

        down.start()

        @pl.when(blk < blocks - 1)
        def _():
            up.start()

        ahead.start()
        behind.start()

    base = (blk * 4).astype(jnp.float32) + 0.5

    def radius(j):
        return base + float(j)

    def own(j):
        r = radius(j)
        rate = STEP / r
        for h in (0, 32):
            rows = slice(h, h + 32)
            q = [u[f, 2 + j, rows] for f in range(FIELDS)]
            ur, ut, uz, p = primitives(q)
            e = q[4] + p
            cross = q[1] * ut
            swirl = q[2] * ut + p
            radial = [q[1], q[1] * ur + p, cross, q[3] * ur, e * ur]
            azimuth = [q[2], cross, swirl, q[3] * ut, e * ut]
            axial = [q[3], q[1] * uz, q[2] * uz, q[3] * uz + p, e * uz]
            grown = [q[0], q[1] + rate * swirl, q[2] - rate * cross, q[3], q[4]]
            for f in range(FIELDS):
                rf[f, 2 + j, rows] = r * radial[f]
                gs[f, j, 16 + h : 48 + h] = azimuth[f]
                sb[f, j, rows] = grown[f]
                high, low = split(axial[f])
                hh[j, 64 * f + h : 64 * f + h + 32, 0:128] = high
                hh[j, 64 * f + h : 64 * f + h + 32, 128:256] = low
        zd[j] = product(hh[j], dz[...])

    def far_flux(c):
        r = base + float(c - 2)
        for h in (0, 32):
            rows = slice(h, h + 32)
            q = [u[f, c, rows] for f in range(FIELDS)]
            ur, _, _, p = primitives(q)
            radial = [q[1], q[1] * ur + p, q[2] * ur, q[3] * ur, (q[4] + p) * ur]
            for f in range(FIELDS):
                rf[f, c, rows] = r * radial[f]

    turn = STEP / (12.0 * 2.0 * math.pi / (64 * sectors))

    def slope_angle(f, j, start, count):
        def part(offset):
            return gs[f, j, start + 16 + offset : start + 16 + offset + count]

        return (part(-2) - part(2)) + 8.0 * (part(1) - part(-1))

    def advance(j):
        kr = (STEP / 12.0) / radius(j)
        kt = turn / radius(j)
        for f in range(FIELDS):
            for h in (0, 32):
                rows = slice(h, h + 32)
                rad = (rf[f, j, rows] - rf[f, j + 4, rows]) + 8.0 * (rf[f, j + 3, rows] - rf[f, j + 1, rows])
                sg[f, j, rows] = (
                    sb[f, j, rows] - kr * rad - kt * slope_angle(f, j, h, 32) - (STEP / 12.0) * zd[j, 64 * f + h : 64 * f + h + 32]
                )

    def edges(j):
        kt = turn / radius(j)
        for f in range(FIELDS):
            sg[f, j, 64:72] = -kt * (slope_angle(f, j, 64, 8) + slope_angle(f, j, -8, 8))

    def short(f, j, start, count):
        parts = product(small[:, 0:count], jnp.concatenate(split(sg[f, j, start : start + count]), 1))
        parts = parts[0:RANK] + parts[RANK : 2 * RANK]
        return parts[:, 0:128] + parts[:, 128:256]

    def pack(j):
        for f in range(FIELDS):
            sides = [short(f, j, 0, 80)] + ([short(f, j, 80, 64)] if j < 2 else [])
            for n, values in enumerate(sides):
                if f < 4:
                    yw[f, j, RANK * n : RANK * n + RANK] = values
                else:
                    for q, part in enumerate(exchanged([values[8 * g : 8 * g + 8] for g in range(4)])):
                        pk[j, q, 8 * n : 8 * n + 8] = part

    def shifted(dx, dy):
        return lax.rem(y + dy, 4) * 4 + lax.rem(x + dx, 4)

    def home(target):
        return jnp.where(target == 0, 1, 0)

    def forward(target, slot, rows):
        f, j, _ = units_of(target)
        return remote(yw.at[f, j, 0:rows], rx.at[az, 0:rows], fs.at[0, slot], fr.at[0, az], home(target), target)

    def forward_quarter(target, slot, rows):
        q, _, j = units_of(target)
        return remote(pk.at[j, q, 0:rows], rq.at[az, 0:rows], fs.at[1, slot], fr.at[1, az], home(target), target)

    def forward_all(inner, act):
        for i, (dx, dy) in enumerate(OFFSETS + [(0, 0)]):
            target = shifted(dx, dy)
            whole = units_of(target)[1] < 2 if inner else units_of(target)[1] >= 2
            away = True if dx or dy else apart

            @pl.when(whole & away)
            def _():
                act(forward(target, i, 2 * RANK if inner else RANK))

            @pl.when(jnp.logical_not(whole) & away)
            def _():
                act(forward_quarter(target, i, 16 if inner else 8))

    my_f, my_j, my_quarter = units_of(az)
    my_inner = my_j < 2

    @pl.when(first)
    def _():
        for c in (4, 5):
            far_flux(c)
        for j in range(2):
            own(j)
        for copy in fetch[:2]:
            copy.wait()
        for j in range(2):
            advance(j)
            edges(j)
            kr = (STEP / 12.0) / radius(j)
            for f in range(FIELDS):
                inner = rf[f, 3] - 8.0 * rf[f, 2] if j == 0 else rf[f, 2]
                sg[f, j, 80:144] = (-SIGN[f] * kr) * inner
            pack(j)
        pl.semaphore_wait(barrier, sectors)
        forward_all(True, lambda c: c.start())
        up.start()
        for j in range(2, 4):
            own(j)

    @pl.when(blk > 0)
    def _():
        for j in range(4):
            own(j)
        ahead.wait_recv()
        behind.wait_recv()
        for side in range(2):
            for a in range(2):
                q = [halo[side, f, a] for f in range(FIELDS)]
                _, ut, _, p = primitives(q)
                azimuth = [q[2], q[1] * ut, q[2] * ut + p, q[3] * ut, (q[4] + p) * ut]
                row = (14 if side == 0 else 80) + a
                for f in range(FIELDS):
                    for j in range(4):
                        gs[f, j, row : row + 1] = azimuth[f][j : j + 1]
        up.wait_recv()
        for c in range(2):
            far_flux(c)

    @pl.when(last)
    def _():
        for f in range(FIELDS):
            for c in (6, 7):
                u[f, c] = u[f, 5]

    @pl.when(blk < blocks - 1)
    def _():
        down.wait_recv()

    for c in (6, 7):
        far_flux(c)

    def plain(j):
        return pltpu.make_async_copy(sg.at[:, j, 0:64], out.at[:, j], out_sem.at[j])

    @pl.when(first)
    def _():
        for j in range(2, 4):
            advance(j)
            edges(j)
            pack(j)
        forward_all(False, lambda c: c.start())

    @pl.when(blk > 0)
    def _():
        for j in range(4):
            advance(j)
            plain(j).start()

    def back(dx, dy):
        target = shifted(dx, dy)
        return remote(kp.at[target], zin.at[my_f, my_j], bs.at[0, 4 * dy + dx], br.at[0, az], 0, target)

    def back_quarter(dx, dy):
        target = shifted(dx, dy)
        return remote(kq.at[target], qin.at[my_quarter, my_f], bs.at[1, 4 * dy + dx], br.at[1, az], 0, target)

    @pl.when(owner)
    def _():
        for whole_inner in (True, False):
            rows, few = (2 * RANK, 8) if whole_inner else (RANK, 16)

            @pl.when(my_inner if whole_inner else jnp.logical_not(my_inner))
            def _(rows=rows, few=few):
                mine = [
                    pltpu.make_async_copy(yw.at[my_f, my_j, 0:rows], rx.at[az, 0:rows], own_sem.at[0]),
                    pltpu.make_async_copy(pk.at[my_quarter, my_f, 0:few], rq.at[az, 0:few], own_sem.at[1]),
                ]

                def arrived(s):
                    remote(yw.at[0, 0, 0:rows], rx.at[s, 0:rows], fs.at[0, 0], fr.at[0, s], 0, s).wait_recv()
                    remote(pk.at[0, 0, 0:few], rq.at[s, 0:few], fs.at[1, 0], fr.at[1, s], 0, s).wait_recv()

                @pl.when(first)
                def _():
                    for copy in mine:
                        copy.start()
                    for copy in mine:
                        copy.wait()

                @pl.when(blk > 0)
                def _():
                    arrived(az)

                for i in others:
                    arrived(at(i))

                group = lax.broadcasted_iota(jnp.int32, (16, 128), 1) // 32

                def gather(n, carry):
                    pair = (2 * n, 2 * n + 1)
                    across = [lax.rem(s + sectors // 2, sectors) for s in pair]
                    quarter = jnp.concatenate([rq[s, 0:8] for s in pair], 0)
                    if few == 16:
                        quarter = quarter + jnp.concatenate([rq[s, 8:16] for s in across], 0)
                    for g in range(4):
                        value = jnp.concatenate([rx[s, 8 * g : 8 * g + 8] for s in pair], 0)
                        if rows == 2 * RANK:
                            value = value + jnp.concatenate(
                                [rx[s, RANK + 8 * g : RANK + 8 * g + 8] for s in across], 0
                            )
                        to = pl.ds(pl.multiple_of(128 * g + n * 16, 16), 16)
                        high, low = split(value)
                        xs[to, 0:128] = high
                        xs[to, 128:256] = low
                        high, low = split(jnp.where(group == g, quarter, 0.0))
                        xs[to, 256:384] = high
                        xs[to, 384:512] = low
                    return carry

                lax.fori_loop(0, sectors // 2, gather, 0, unroll=2)

        for copy in fetch[2:]:
            copy.wait()
        order = lax.rem(lax.broadcasted_iota(jnp.int32, (2 * MMAX, 128), 0), MMAX)
        scale = jnp.where(order == 0, 1.0, 2.0) / float(64 * sectors)
        sides = []
        for n, cycle in ((0, my_j), (256, my_quarter)):
            parts = product(forth[0:256], xs[0:128, n : n + 256])
            for g in range(1, 4):
                parts = parts + product(
                    forth[256 * g : 256 * g + 256], xs[128 * g : 128 * g + 128, n : n + 256]
                )
            parts = parts[0:128] + parts[128:256]
            coef = parts[:, 0:128] + parts[:, 128:256]
            if n:
                coef = coef + pltpu.roll(coef, 64, 1)
                coef = coef + pltpu.roll(coef, 32, 1)
            sides.extend(split(coef * jnp.where(order < cut[cycle], scale, 0.0)))
        both = jnp.concatenate(sides, 1)
        both = jnp.concatenate([both, both], 0)
        group = lax.broadcasted_iota(jnp.int32, (8, 128), 1) // 32
        for dy in (2, 1, 3, 0):
            yy = lax.rem(y + dy, 4)
            kept = product(home_again[pl.ds(pl.multiple_of(yy * 128, 128), 128)], both)
            whole = kept[:, 0:128] + kept[:, 128:256]
            part = kept[:, 256:384] + kept[:, 384:512]
            for i in range(4):
                kp[yy * 4 + i] = whole[RANK * i : RANK * i + RANK]
                packed = part[RANK * i : RANK * i + 8]
                for g in range(1, 4):
                    packed = jnp.where(group == g, part[RANK * i + 8 * g : RANK * i + 8 * g + 8], packed)
                kq[yy * 4 + i] = packed
            for dx in (2, 1, 3, 0):
                if dx or dy:
                    back_quarter(dx, dy).start()
                    back(dx, dy).start()

        @pl.when(blk > 0)
        def _():
            back_quarter(0, 0).start()
            back(0, 0).start()

        @pl.when(first)
        def _():
            mine = [
                pltpu.make_async_copy(kp.at[az], zin.at[my_f, my_j], own_sem.at[0]),
                pltpu.make_async_copy(kq.at[az], qin.at[my_quarter, my_f], own_sem.at[1]),
            ]
            for copy in mine:
                copy.start()
            for copy in mine:
                copy.wait()

    @pl.when(first)
    def _():
        def quarter_back(o):
            q, _, j = units_of(o)
            remote(kq.at[0], qin.at[j, q], bs.at[1, 0], br.at[1, o], home(o), o).wait_recv()

        def whole_back(o):
            f, j, _ = units_of(o)
            remote(kp.at[0], zin.at[f, j], bs.at[0, 0], br.at[0, o], home(o), o).wait_recv()

        for i in others:
            quarter_back(at(i))

        @pl.when(apart)
        def _():
            quarter_back(az)
            whole_back(az)

        def full(f, j, values):
            both = jnp.concatenate(split(values), 1)
            parts = product(large[:, 0 : 2 * RANK], jnp.concatenate([both, both], 0))
            sg[f, j, 0:64] = parts[:, 0:128] + parts[:, 128:256]

        for j in range(4):
            full(4, j, jnp.concatenate(exchanged([qin[j, q] for q in range(4)]), 0))
        for i in others:
            whole_back(at(i))
        for j in range(4):
            for f in range(4):
                full(f, j, zin[f, j])
            plain(j).start()
        for j in range(4):
            plain(j).wait()
        up.wait_send()
        forward_all(True, lambda c: c.wait_send())
        forward_all(False, lambda c: c.wait_send())

    @pl.when(owner)
    def _():
        for dx, dy in OFFSETS:
            back(dx, dy).wait_send()
            back_quarter(dx, dy).wait_send()

        @pl.when(blk > 0)
        def _():
            back(0, 0).wait_send()
            back_quarter(0, 0).wait_send()

    @pl.when(blk > 0)
    def _():
        for j in range(4):
            plain(j).wait()
        down.wait_send()

        @pl.when(blk < blocks - 1)
        def _():
            up.wait_send()

        ahead.wait_send()
        behind.wait_send()


def place(held, out, sems):
    copies = [pltpu.make_async_copy(held.at[:, j], out.at[:, :, j], sems.at[j]) for j in range(4)]
    for copy in copies:
        copy.start()
    for copy in copies:
        copy.wait()


def shards(cut_table, blocks, sectors, state, cutoffs):
    points = state.shape[3]
    f32, bf16 = jnp.float32, jnp.bfloat16
    dma = pltpu.SemaphoreType.DMA
    anywhere = pl.BlockSpec(memory_space=pl.ANY)
    held = pl.pallas_call(
        functools.partial(kernel, blocks, sectors),
        out_shape=jax.ShapeDtypeStruct((FIELDS, 4, 64, points), f32),
        in_specs=[pl.BlockSpec(memory_space=pltpu.SMEM)] + [anywhere] * 2,
        out_specs=anywhere,
        scratch_shapes=[
            pltpu.VMEM((FIELDS, 8, 64, points), f32),
            pltpu.VMEM((FIELDS, 8, 64, points), f32),
            pltpu.VMEM((FIELDS, 4, 96, points), f32),
            pltpu.VMEM((4, FIELDS * 64, 2 * points), bf16),
            pltpu.VMEM((4, FIELDS * 64, points), f32),
            pltpu.VMEM((FIELDS, 4, 64, points), f32),
            pltpu.VMEM((FIELDS, 4, 144, points), f32),
            pltpu.VMEM((2, FIELDS, 2, 4, points), f32),
            pltpu.VMEM((4, 4, 2 * RANK, points), f32),
            pltpu.VMEM((sectors, 2 * RANK, points), f32),
            pltpu.VMEM((sectors, 16, points), f32),
            pltpu.VMEM((4, 4, 16, points), f32),
            pltpu.VMEM((RANK * sectors, 4 * points), bf16),
            pltpu.VMEM((sectors, RANK, points), f32),
            pltpu.VMEM((sectors, 8, points), f32),
            pltpu.VMEM((4, 4, 8, points), f32),
            pltpu.VMEM((4, 4, RANK, points), f32),
            pltpu.VMEM((2 * RANK, 128), bf16),
            pltpu.VMEM((64, 128), bf16),
            pltpu.VMEM((16 * MMAX, 128), bf16),
            pltpu.VMEM((RANK * sectors, 4 * MMAX), bf16),
            pltpu.VMEM((2 * points, points), bf16),
            dma((4,)),
            dma((5,)),
            dma((4,)),
            dma((4,)),
            dma((2, sectors)),
            dma((2, sectors)),
            dma((2, sectors)),
            dma((2, sectors)),
            dma((2,)),
            dma((4,)),
        ],
        compiler_params=pltpu.CompilerParams(
            collective_id=0, has_side_effects=True, vmem_limit_bytes=LIMIT_MIB * 1024 * 1024
        ),
        name="section",
    )(cutoffs, state, jnp.asarray(cut_table))
    return pl.pallas_call(
        place,
        out_shape=jax.ShapeDtypeStruct(state.shape, f32),
        in_specs=[anywhere],
        out_specs=anywhere,
        scratch_shapes=[dma((4,))],
        compiler_params=pltpu.CompilerParams(vmem_limit_bytes=1024 * 1024),
        name="place",
    )(held)


def solution(mesh):
    blocks, sectors = mesh.shape["blk"], mesh.shape["az"]
    placed = (P(None, "az", "blk", None), P())
    return jax.shard_map(
        functools.partial(shards, tables(64 * sectors), blocks, sectors),
        mesh=mesh,
        in_specs=placed,
        out_specs=P(None, "az", "blk", None),
        check_vma=False,
    )
```

```python
import functools
import math

import jax
import jax.numpy as jnp
import ml_dtypes
import numpy as np
from jax import lax
from jax.experimental import pallas as pl
from jax.experimental.pallas import tpu as pltpu
from jax.sharding import PartitionSpec as P

MESH = pl.DeviceIdType.MESH
FIELDS = 5
MMAX = 64
RANK = 24
GROUPS = RANK // 8
GAS = 0.4
STEP = 0.025
SIGN = (1.0, -1.0, -1.0, 1.0, 1.0)
LIMIT_MIB = 53


OFFSETS = sorted(
    ((dx, dy) for dx in range(4) for dy in range(4) if dx or dy),
    key=lambda o: -(min(o[0], 4 - o[0]) + min(o[1], 4 - o[1])),
)


def halves(values):
    high = values.astype(ml_dtypes.bfloat16)
    return high, (values - high.astype(np.float64)).astype(ml_dtypes.bfloat16)


def tables(total):
    window = np.arange(-2, 66)
    place = np.arange(68.0)
    side = place[1:] * (68.0 - place[1:]) / 2.0
    inner = (33.5 - place) ** 2 * math.cos(2.0 * math.pi * MMAX / total)
    _, basis = np.linalg.eigh(np.diag(inner) + np.diag(side, 1) + np.diag(side, -1))
    basis = basis[:, : -RANK - 1 : -1]
    basis = basis * np.sign(basis[-1:])
    rows = np.zeros((80, RANK))
    rows[window % 72] = basis
    modes = np.arange(MMAX)[:, None]
    angle = modes * window[None, :] * (2.0 * math.pi / total)
    even, odd = np.cos(angle) @ basis, np.sin(angle) @ basis
    turn = (modes * 64 * np.arange(total // 64)[None, :]) % total * (2.0 * math.pi / total)
    cos_t, sin_t = np.cos(turn)[:, :, None], np.sin(turn)[:, :, None]
    even, odd = even[:, None, :], odd[:, None, :]
    both = np.concatenate([cos_t * even - sin_t * odd, sin_t * even + cos_t * odd], 0)
    both = both.reshape(2 * MMAX, -1)
    forth = np.concatenate(halves(both), 0)
    grouped = forth.reshape(4 * MMAX, -1, GROUPS, 8).transpose(2, 0, 1, 3).reshape(4 * MMAX * GROUPS, -1)
    shrink = np.concatenate(halves(rows.T), 0)
    grow = np.concatenate(halves(rows[:64]), 1)
    out = np.zeros((4096, 128), ml_dtypes.bfloat16)
    count = len(forth.T)
    out[0 : len(grouped)] = grouped
    out[1024 : 1024 + count], out[1536 : 1536 + count] = forth.T[:, 0:128], forth.T[:, 128:256]
    out[2048 : 2048 + len(shrink), 0:80], out[2112:2176, 0 : 2 * RANK] = shrink, grow
    return out


def units_of(az):
    t = lax.rem(az + az // 4, 4)
    odd, upper = lax.rem(t, 2), t // 2
    return az // 4, 2 * odd + upper, 2 * (1 - odd) + upper


def exchanged(pieces):
    group = lax.broadcasted_iota(jnp.int32, pieces[0].shape, 1) // 32
    out = []
    for a in range(4):
        value = pieces[a]
        for b in range(4):
            if b != a:
                value = jnp.where(group == b, pltpu.roll(pieces[b], (32 * (b - a)) % 128, 1), value)
        out.append(value)
    return out


def split(value):
    high = value.astype(jnp.bfloat16)
    return high, (value - high.astype(jnp.float32)).astype(jnp.bfloat16)


def product(a, b):
    return jnp.dot(a, b, preferred_element_type=jnp.float32)


def axial_matrix():
    point = lax.rem(lax.broadcasted_iota(jnp.int32, (256, 128), 0), 128)
    at = lax.broadcasted_iota(jnp.int32, (256, 128), 1)
    total = jnp.zeros((256, 128), jnp.float32)
    for offset, c in ((-2, 1.0), (-1, -8.0), (1, 8.0), (2, -1.0)):
        total = total + jnp.where(point == jnp.clip(at + offset, 0, 127), c, 0.0)
    return total.astype(jnp.bfloat16)


def primitives(q):
    inv = 1.0 / q[0]
    ur, ut, uz = q[1] * inv, q[2] * inv, q[3] * inv
    p = GAS * (q[4] - 0.5 * (q[1] * ur + q[2] * ut + q[3] * uz))
    return ur, ut, uz, p


def kernel(blocks, sectors, cut, state, transforms, out, u, rf, gs, hh, zd, sb, sg, halo,
           yw, rx, rq, pk, xs, kp, kq, qin, zin, small, large, forth, home_again, dz, load_sem, table_sem, hs, hr, fs, fr, bs, br, own_sem, out_sem):
    blk = lax.axis_index("blk")
    az = lax.axis_index("az")
    first = blk == 0
    last = blk == blocks - 1
    x, y = lax.rem(az, 4), az // 4
    apart = az == 0
    owner = (first & jnp.logical_not(apart)) | ((blk == 1) & apart)
    others = range(1, sectors)

    def at(i):
        return lax.rem(az + i, sectors)

    loads = [pltpu.make_async_copy(state.at[:, :, j], u.at[:, 2 + j], load_sem.at[j]) for j in range(4)]
    for copy in loads:
        copy.start()
    fetch = [
        pltpu.make_async_copy(transforms.at[a:b], to, table_sem.at[n])
        for n, (a, b, to) in enumerate(
            (
                (2048, 2048 + 2 * RANK, small),
                (2112, 2176, large),
                (0, 4 * MMAX * GROUPS, forth),
                (1024, 1024 + RANK * sectors, home_again.at[:, 0:128]),
                (1536, 1536 + RANK * sectors, home_again.at[:, 128:256]),
            )
        )
    ]

    barrier = pltpu.get_barrier_semaphore()

    def greet(b, a):
        pl.semaphore_signal(barrier, inc=1, device_id=(b, a), device_id_type=MESH)

    @pl.when(first)
    def _():
        greet(1, az)

        @pl.when(jnp.logical_not(apart))
        def _():
            for i in others:
                greet(0, at(i))

    @pl.when((blk == 1) & apart)
    def _():
        for i in others:
            greet(0, at(i))

    @pl.when(first)
    def _():
        for copy in fetch[:2]:
            copy.start()

    @pl.when(owner)
    def _():
        for copy in fetch[2:]:
            copy.start()

    @pl.when(blk > 0)
    def _():
        greet(blk - 1, az)
        greet(blk, at(1))
        greet(blk, at(sectors - 1))

        @pl.when(blk < blocks - 1)
        def _():
            greet(blk + 1, az)

    def remote(src, dst, send, recv, b, a):
        return pltpu.make_async_remote_copy(
            src_ref=src, dst_ref=dst, send_sem=send, recv_sem=recv, device_id=(b, a), device_id_type=MESH
        )

    up = remote(u.at[:, 4:6], u.at[:, 0:2], hs.at[0], hr.at[0], jnp.minimum(blk + 1, blocks - 1), az)
    down = remote(u.at[:, 2:4], u.at[:, 6:8], hs.at[1], hr.at[1], jnp.maximum(blk - 1, 0), az)
    ahead = remote(state.at[:, 62:64], halo.at[0], hs.at[2], hr.at[2], blk, at(1))
    behind = remote(state.at[:, 0:2], halo.at[1], hs.at[3], hr.at[3], blk, at(sectors - 1))

    dz[...] = axial_matrix()

    @pl.when(first)
    def _():
        zero = jnp.zeros((64, 128), jnp.float32)
        for f in range(FIELDS):
            for c in range(2):
                rf[f, c] = zero
            for j in range(4):
                gs[f, j, 0:16] = zero[:16]
                gs[f, j, 80:96] = zero[:16]
                sg[f, j, 72:80] = zero[:8]

    for copy in loads:
        copy.wait()

    @pl.when(blk > 0)
    def _():
        @pl.when(blk < blocks - 1)
        def _():
            pl.semaphore_wait(barrier, 4)

        @pl.when(last)
        def _():
            pl.semaphore_wait(barrier, 3)

        down.start()

        @pl.when(blk < blocks - 1)
        def _():
            up.start()

        ahead.start()
        behind.start()

    base = (blk * 4).astype(jnp.float32) + 0.5

    def radius(j):
        return base + float(j)

    def own(j):
        r = radius(j)
        rate = STEP / r
        for h in (0, 32):
            rows = slice(h, h + 32)
            q = [u[f, 2 + j, rows] for f in range(FIELDS)]
            ur, ut, uz, p = primitives(q)
            e = q[4] + p
            cross = q[1] * ut
            swirl = q[2] * ut + p
            radial = [q[1], q[1] * ur + p, cross, q[3] * ur, e * ur]
            azimuth = [q[2], cross, swirl, q[3] * ut, e * ut]
            axial = [q[3], q[1] * uz, q[2] * uz, q[3] * uz + p, e * uz]
            grown = [q[0], q[1] + rate * swirl, q[2] - rate * cross, q[3], q[4]]
            for f in range(FIELDS):
                rf[f, 2 + j, rows] = r * radial[f]
                gs[f, j, 16 + h : 48 + h] = azimuth[f]
                sb[f, j, rows] = grown[f]
                high, low = split(axial[f])
                hh[j, 64 * f + h : 64 * f + h + 32, 0:128] = high
                hh[j, 64 * f + h : 64 * f + h + 32, 128:256] = low
        zd[j] = product(hh[j], dz[...])

    def far_flux(c):
        r = base + float(c - 2)
        for h in (0, 32):
            rows = slice(h, h + 32)
            q = [u[f, c, rows] for f in range(FIELDS)]
            ur, _, _, p = primitives(q)
            radial = [q[1], q[1] * ur + p, q[2] * ur, q[3] * ur, (q[4] + p) * ur]
            for f in range(FIELDS):
                rf[f, c, rows] = r * radial[f]

    turn = STEP / (12.0 * 2.0 * math.pi / (64 * sectors))

    def slope_angle(f, j, start, count):
        def part(offset):
            return gs[f, j, start + 16 + offset : start + 16 + offset + count]

        return (part(-2) - part(2)) + 8.0 * (part(1) - part(-1))

    def advance(j):
        kr = (STEP / 12.0) / radius(j)
        kt = turn / radius(j)
        for f in range(FIELDS):
            for h in (0, 32):
                rows = slice(h, h + 32)
                rad = (rf[f, j, rows] - rf[f, j + 4, rows]) + 8.0 * (rf[f, j + 3, rows] - rf[f, j + 1, rows])
                sg[f, j, rows] = (
                    sb[f, j, rows] - kr * rad - kt * slope_angle(f, j, h, 32) - (STEP / 12.0) * zd[j, 64 * f + h : 64 * f + h + 32]
                )

    def edges(j):
        kt = turn / radius(j)
        for f in range(FIELDS):
            sg[f, j, 64:72] = -kt * (slope_angle(f, j, 64, 8) + slope_angle(f, j, -8, 8))

    def short(f, j, start, count):
        parts = product(small[:, 0:count], jnp.concatenate(split(sg[f, j, start : start + count]), 1))
        parts = parts[0:RANK] + parts[RANK : 2 * RANK]
        return parts[:, 0:128] + parts[:, 128:256]

    def pack(j):
        for f in range(FIELDS):
            sides = [short(f, j, 0, 80)] + ([short(f, j, 80, 64)] if j < 2 else [])
            for n, values in enumerate(sides):
                if f < 4:
                    yw[f, j, RANK * n : RANK * n + RANK] = values
                else:
                    groups = [values[8 * g : 8 * g + 8] for g in range(GROUPS)]
                    groups += [jnp.zeros((8, 128), jnp.float32)] * (4 - GROUPS)
                    for q, part in enumerate(exchanged(groups)):
                        pk[j, q, 8 * n : 8 * n + 8] = part

    def shifted(dx, dy):
        return lax.rem(y + dy, 4) * 4 + lax.rem(x + dx, 4)

    def home(target):
        return jnp.where(target == 0, 1, 0)

    def forward(target, slot, rows):
        f, j, _ = units_of(target)
        return remote(yw.at[f, j, 0:rows], rx.at[az, 0:rows], fs.at[0, slot], fr.at[0, az], home(target), target)

    def forward_quarter(target, slot, rows):
        q, _, j = units_of(target)
        return remote(pk.at[j, q, 0:rows], rq.at[az, 0:rows], fs.at[1, slot], fr.at[1, az], home(target), target)

    def forward_all(inner, act):
        for i, (dx, dy) in enumerate(OFFSETS + [(0, 0)]):
            target = shifted(dx, dy)
            whole = units_of(target)[1] < 2 if inner else units_of(target)[1] >= 2
            away = True if dx or dy else apart

            @pl.when(whole & away)
            def _():
                act(forward(target, i, 2 * RANK if inner else RANK))

            @pl.when(jnp.logical_not(whole) & away)
            def _():
                act(forward_quarter(target, i, 16 if inner else 8))

    my_f, my_j, my_quarter = units_of(az)
    my_inner = my_j < 2

    @pl.when(first)
    def _():
        for c in (4, 5):
            far_flux(c)
        for j in range(2):
            own(j)
        for copy in fetch[:2]:
            copy.wait()
        for j in range(2):
            advance(j)
            edges(j)
            kr = (STEP / 12.0) / radius(j)
            for f in range(FIELDS):
                inner = rf[f, 3] - 8.0 * rf[f, 2] if j == 0 else rf[f, 2]
                sg[f, j, 80:144] = (-SIGN[f] * kr) * inner
            pack(j)
        pl.semaphore_wait(barrier, sectors)
        forward_all(True, lambda c: c.start())
        up.start()
        for j in range(2, 4):
            own(j)

    @pl.when(blk > 0)
    def _():
        for j in range(4):
            own(j)
        ahead.wait_recv()
        behind.wait_recv()
        for side in range(2):
            for a in range(2):
                q = [halo[side, f, a] for f in range(FIELDS)]
                _, ut, _, p = primitives(q)
                azimuth = [q[2], q[1] * ut, q[2] * ut + p, q[3] * ut, (q[4] + p) * ut]
                row = (14 if side == 0 else 80) + a
                for f in range(FIELDS):
                    for j in range(4):
                        gs[f, j, row : row + 1] = azimuth[f][j : j + 1]
        up.wait_recv()
        for c in range(2):
            far_flux(c)

    @pl.when(last)
    def _():
        for f in range(FIELDS):
            for c in (6, 7):
                u[f, c] = u[f, 5]

    @pl.when(blk < blocks - 1)
    def _():
        down.wait_recv()

    for c in (6, 7):
        far_flux(c)

    def plain(j):
        return pltpu.make_async_copy(sg.at[:, j, 0:64], out.at[:, j], out_sem.at[0, j])

    @pl.when(first)
    def _():
        for j in range(2, 4):
            advance(j)
            edges(j)
            pack(j)
        forward_all(False, lambda c: c.start())

    @pl.when(blk > 0)
    def _():
        for j in range(4):
            advance(j)
            plain(j).start()

    def back(dx, dy):
        target = shifted(dx, dy)
        return remote(kp.at[target], zin.at[my_f, my_j], bs.at[0, 4 * dy + dx], br.at[0, az], 0, target)

    def back_quarter(dx, dy):
        target = shifted(dx, dy)
        return remote(kq.at[target], qin.at[my_quarter, my_f], bs.at[1, 4 * dy + dx], br.at[1, az], 0, target)

    @pl.when(owner)
    def _():
        for whole_inner in (True, False):
            rows, few = (2 * RANK, 8) if whole_inner else (RANK, 16)

            @pl.when(my_inner if whole_inner else jnp.logical_not(my_inner))
            def _(rows=rows, few=few):
                mine = [
                    pltpu.make_async_copy(yw.at[my_f, my_j, 0:rows], rx.at[az, 0:rows], own_sem.at[0]),
                    pltpu.make_async_copy(pk.at[my_quarter, my_f, 0:few], rq.at[az, 0:few], own_sem.at[1]),
                ]

                def arrived(s):
                    remote(yw.at[0, 0, 0:rows], rx.at[s, 0:rows], fs.at[0, 0], fr.at[0, s], 0, s).wait_recv()
                    remote(pk.at[0, 0, 0:few], rq.at[s, 0:few], fs.at[1, 0], fr.at[1, s], 0, s).wait_recv()

                @pl.when(first)
                def _():
                    for copy in mine:
                        copy.start()
                    for copy in mine:
                        copy.wait()

                @pl.when(blk > 0)
                def _():
                    arrived(az)

                for i in others:
                    arrived(at(i))

                group = lax.broadcasted_iota(jnp.int32, (16, 128), 1) // 32

                def gather(n, carry):
                    pair = (2 * n, 2 * n + 1)
                    across = [lax.rem(s + sectors // 2, sectors) for s in pair]
                    quarter = jnp.concatenate([rq[s, 0:8] for s in pair], 0)
                    if few == 16:
                        quarter = quarter + jnp.concatenate([rq[s, 8:16] for s in across], 0)
                    for g in range(GROUPS):
                        value = jnp.concatenate([rx[s, 8 * g : 8 * g + 8] for s in pair], 0)
                        if rows == 2 * RANK:
                            value = value + jnp.concatenate(
                                [rx[s, RANK + 8 * g : RANK + 8 * g + 8] for s in across], 0
                            )
                        to = pl.ds(pl.multiple_of(128 * g + n * 16, 16), 16)
                        high, low = split(value)
                        xs[to, 0:128] = high
                        xs[to, 128:256] = low
                        high, low = split(jnp.where(group == g, quarter, 0.0))
                        xs[to, 256:384] = high
                        xs[to, 384:512] = low
                    return carry

                lax.fori_loop(0, sectors // 2, gather, 0, unroll=2)

        for copy in fetch[2:]:
            copy.wait()
        order = lax.rem(lax.broadcasted_iota(jnp.int32, (2 * MMAX, 128), 0), MMAX)
        scale = jnp.where(order == 0, 1.0, 2.0) / float(64 * sectors)
        sides = []
        for n, cycle in ((0, my_j), (256, my_quarter)):
            parts = product(forth[0:256], xs[0:128, n : n + 256])
            for g in range(1, GROUPS):
                parts = parts + product(
                    forth[256 * g : 256 * g + 256], xs[128 * g : 128 * g + 128, n : n + 256]
                )
            parts = parts[0:128] + parts[128:256]
            coef = parts[:, 0:128] + parts[:, 128:256]
            if n:
                coef = coef + pltpu.roll(coef, 64, 1)
                coef = coef + pltpu.roll(coef, 32, 1)
            sides.extend(split(coef * jnp.where(order < cut[cycle], scale, 0.0)))
        both = jnp.concatenate(sides, 1)
        both = jnp.concatenate([both, both], 0)
        group = lax.broadcasted_iota(jnp.int32, (8, 128), 1) // 32
        for dy in (2, 1, 3, 0):
            yy = lax.rem(y + dy, 4)
            kept = product(home_again[pl.ds(pl.multiple_of(yy * 4 * RANK, 4 * RANK), 4 * RANK)], both)
            whole = kept[:, 0:128] + kept[:, 128:256]
            part = kept[:, 256:384] + kept[:, 384:512]
            for i in range(4):
                kp[yy * 4 + i] = whole[RANK * i : RANK * i + RANK]
                packed = part[RANK * i : RANK * i + 8]
                for g in range(1, GROUPS):
                    packed = jnp.where(group == g, part[RANK * i + 8 * g : RANK * i + 8 * g + 8], packed)
                kq[yy * 4 + i] = packed
            for dx in (2, 1, 3, 0):
                if dx or dy:
                    back_quarter(dx, dy).start()
                    back(dx, dy).start()

        @pl.when(blk > 0)
        def _():
            back_quarter(0, 0).start()
            back(0, 0).start()

        @pl.when(first)
        def _():
            mine = [
                pltpu.make_async_copy(kp.at[az], zin.at[my_f, my_j], own_sem.at[0]),
                pltpu.make_async_copy(kq.at[az], qin.at[my_quarter, my_f], own_sem.at[1]),
            ]
            for copy in mine:
                copy.start()
            for copy in mine:
                copy.wait()

    @pl.when(first)
    def _():
        def quarter_back(o):
            q, _, j = units_of(o)
            remote(kq.at[0], qin.at[j, q], bs.at[1, 0], br.at[1, o], home(o), o).wait_recv()

        def whole_back(o):
            f, j, _ = units_of(o)
            remote(kp.at[0], zin.at[f, j], bs.at[0, 0], br.at[0, o], home(o), o).wait_recv()

        def full(f, j, values):
            both = jnp.concatenate(split(jnp.concatenate([values, values], 0)), 1)
            parts = product(large[:, 0 : 2 * RANK], both)
            sg[f, j, 0:64] = parts[:, 0:128] + parts[:, 128:256]

        for i in others:
            quarter_back(at(i))

        @pl.when(apart)
        def _():
            quarter_back(az)
            whole_back(az)

        for j in range(4):
            full(4, j, jnp.concatenate(exchanged([qin[j, q] for q in range(4)])[:GROUPS], 0))
        for i in others:
            whole_back(at(i))
        for j in range(4):
            for f in range(4):
                full(f, j, zin[f, j])
            plain(j).start()
        for j in range(4):
            plain(j).wait()
        up.wait_send()
        forward_all(True, lambda c: c.wait_send())
        forward_all(False, lambda c: c.wait_send())

    @pl.when(owner)
    def _():
        for dx, dy in OFFSETS:
            back(dx, dy).wait_send()
            back_quarter(dx, dy).wait_send()

        @pl.when(blk > 0)
        def _():
            back(0, 0).wait_send()
            back_quarter(0, 0).wait_send()

    @pl.when(blk > 0)
    def _():
        for j in range(4):
            plain(j).wait()
        down.wait_send()

        @pl.when(blk < blocks - 1)
        def _():
            up.wait_send()

        ahead.wait_send()
        behind.wait_send()


def place(held, out, sems):
    copies = [pltpu.make_async_copy(held.at[:, j], out.at[:, :, j], sems.at[j]) for j in range(4)]
    for copy in copies:
        copy.start()
    for copy in copies:
        copy.wait()


def shards(cut_table, blocks, sectors, state, cutoffs):
    points = state.shape[3]
    f32, bf16 = jnp.float32, jnp.bfloat16
    dma = pltpu.SemaphoreType.DMA
    anywhere = pl.BlockSpec(memory_space=pl.ANY)
    held = pl.pallas_call(
        functools.partial(kernel, blocks, sectors),
        out_shape=jax.ShapeDtypeStruct((FIELDS, 4, 64, points), f32),
        in_specs=[pl.BlockSpec(memory_space=pltpu.SMEM)] + [anywhere] * 2,
        out_specs=anywhere,
        scratch_shapes=[
            pltpu.VMEM((FIELDS, 8, 64, points), f32),
            pltpu.VMEM((FIELDS, 8, 64, points), f32),
            pltpu.VMEM((FIELDS, 4, 96, points), f32),
            pltpu.VMEM((4, FIELDS * 64, 2 * points), bf16),
            pltpu.VMEM((4, FIELDS * 64, points), f32),
            pltpu.VMEM((FIELDS, 4, 64, points), f32),
            pltpu.VMEM((FIELDS, 4, 144, points), f32),
            pltpu.VMEM((2, FIELDS, 2, 4, points), f32),
            pltpu.VMEM((4, 4, 2 * RANK, points), f32),
            pltpu.VMEM((sectors, 2 * RANK, points), f32),
            pltpu.VMEM((sectors, 16, points), f32),
            pltpu.VMEM((4, 4, 16, points), f32),
            pltpu.VMEM((RANK * sectors, 4 * points), bf16),
            pltpu.VMEM((sectors, RANK, points), f32),
            pltpu.VMEM((sectors, 8, points), f32),
            pltpu.VMEM((4, 4, 8, points), f32),
            pltpu.VMEM((4, 4, RANK, points), f32),
            pltpu.VMEM((2 * RANK, 128), bf16),
            pltpu.VMEM((64, 128), bf16),
            pltpu.VMEM((4 * MMAX * GROUPS, 128), bf16),
            pltpu.VMEM((RANK * sectors, 4 * MMAX), bf16),
            pltpu.VMEM((2 * points, points), bf16),
            dma((4,)),
            dma((5,)),
            dma((4,)),
            dma((4,)),
            dma((2, sectors)),
            dma((2, sectors)),
            dma((2, sectors)),
            dma((2, sectors)),
            dma((2,)),
            dma((FIELDS, 4)),
        ],
        compiler_params=pltpu.CompilerParams(
            collective_id=0, has_side_effects=True, vmem_limit_bytes=LIMIT_MIB * 1024 * 1024
        ),
        name="section",
    )(cutoffs, state, jnp.asarray(cut_table))
    return pl.pallas_call(
        place,
        out_shape=jax.ShapeDtypeStruct(state.shape, f32),
        in_specs=[anywhere],
        out_specs=anywhere,
        scratch_shapes=[dma((4,))],
        compiler_params=pltpu.CompilerParams(vmem_limit_bytes=1024 * 1024),
        name="place",
    )(held)


def solution(mesh):
    blocks, sectors = mesh.shape["blk"], mesh.shape["az"]
    placed = (P(None, "az", "blk", None), P())
    return jax.shard_map(
        functools.partial(shards, tables(64 * sectors), blocks, sectors),
        mesh=mesh,
        in_specs=placed,
        out_specs=P(None, "az", "blk", None),
        check_vma=False,
    )
```

```python
import functools
import math

import jax
import jax.numpy as jnp
import ml_dtypes
import numpy as np
from jax import lax
from jax.experimental import pallas as pl
from jax.experimental.pallas import tpu as pltpu
from jax.sharding import PartitionSpec as P

MESH = pl.DeviceIdType.MESH
FIELDS = 5
MMAX = 64
RANK = 24
GROUPS = RANK // 8
GAS = 0.4
STEP = 0.025
SIGN = (1.0, -1.0, -1.0, 1.0, 1.0)
LIMIT_MIB = 53


OFFSETS = sorted(
    ((dx, dy) for dx in range(4) for dy in range(4) if dx or dy),
    key=lambda o: -(min(o[0], 4 - o[0]) + min(o[1], 4 - o[1])),
)


def halves(values):
    high = values.astype(ml_dtypes.bfloat16)
    return high, (values - high.astype(np.float64)).astype(ml_dtypes.bfloat16)


def tables(total):
    window = np.arange(-2, 66)
    place = np.arange(68.0)
    side = place[1:] * (68.0 - place[1:]) / 2.0
    inner = (33.5 - place) ** 2 * math.cos(2.0 * math.pi * MMAX / total)
    _, basis = np.linalg.eigh(np.diag(inner) + np.diag(side, 1) + np.diag(side, -1))
    basis = basis[:, : -RANK - 1 : -1]
    basis = basis * np.sign(basis[-1:])
    rows = np.zeros((80, RANK))
    rows[window % 72] = basis
    modes = np.arange(MMAX)[:, None]
    angle = modes * window[None, :] * (2.0 * math.pi / total)
    even, odd = np.cos(angle) @ basis, np.sin(angle) @ basis
    turn = (modes * 64 * np.arange(total // 64)[None, :]) % total * (2.0 * math.pi / total)
    cos_t, sin_t = np.cos(turn)[:, :, None], np.sin(turn)[:, :, None]
    even, odd = even[:, None, :], odd[:, None, :]
    both = np.concatenate([cos_t * even - sin_t * odd, sin_t * even + cos_t * odd], 0)
    both = both.reshape(2 * MMAX, -1)
    forth = np.concatenate(halves(both), 0)
    grouped = forth.reshape(4 * MMAX, -1, GROUPS, 8).transpose(2, 0, 1, 3).reshape(4 * MMAX * GROUPS, -1)
    shrink = np.concatenate(halves(rows.T), 0)
    grow = np.concatenate(halves(rows[:64]), 1)
    out = np.zeros((4096, 128), ml_dtypes.bfloat16)
    count = len(forth.T)
    out[0 : len(grouped)] = grouped
    out[1024 : 1024 + count], out[1536 : 1536 + count] = forth.T[:, 0:128], forth.T[:, 128:256]
    out[2048 : 2048 + len(shrink), 0:80], out[2112:2176, 0 : 2 * RANK] = shrink, grow
    return out


def units_of(az):
    t = lax.rem(az + az // 4, 4)
    odd, upper = lax.rem(t, 2), t // 2
    return az // 4, 2 * odd + upper, 2 * (1 - odd) + upper


def exchanged(pieces):
    group = lax.broadcasted_iota(jnp.int32, pieces[0].shape, 1) // 32
    out = []
    for a in range(4):
        value = pieces[a]
        for b in range(4):
            if b != a:
                value = jnp.where(group == b, pltpu.roll(pieces[b], (32 * (b - a)) % 128, 1), value)
        out.append(value)
    return out


def split(value):
    high = value.astype(jnp.bfloat16)
    return high, (value - high.astype(jnp.float32)).astype(jnp.bfloat16)


def product(a, b):
    return jnp.dot(a, b, preferred_element_type=jnp.float32)


def axial_matrix():
    point = lax.rem(lax.broadcasted_iota(jnp.int32, (256, 128), 0), 128)
    at = lax.broadcasted_iota(jnp.int32, (256, 128), 1)
    total = jnp.zeros((256, 128), jnp.float32)
    for offset, c in ((-2, 1.0), (-1, -8.0), (1, 8.0), (2, -1.0)):
        total = total + jnp.where(point == jnp.clip(at + offset, 0, 127), c, 0.0)
    return total.astype(jnp.bfloat16)


def primitives(q):
    inv = 1.0 / q[0]
    ur, ut, uz = q[1] * inv, q[2] * inv, q[3] * inv
    p = GAS * (q[4] - 0.5 * (q[1] * ur + q[2] * ut + q[3] * uz))
    return ur, ut, uz, p


def kernel(blocks, sectors, cut, state, transforms, out, u, rf, gs, hh, zd, sb, sg, halo,
           yw, rx, rq, pk, xs, kp, kq, qin, zin, small, large, forth, home_again, dz, load_sem, table_sem, hs, hr, fs, fr, bs, br, own_sem, out_sem):
    blk = lax.axis_index("blk")
    az = lax.axis_index("az")
    first = blk == 0
    last = blk == blocks - 1
    x, y = lax.rem(az, 4), az // 4
    apart = az == 0
    owner = (first & jnp.logical_not(apart)) | ((blk == 1) & apart)
    others = range(1, sectors)

    def at(i):
        return lax.rem(az + i, sectors)

    loads = [pltpu.make_async_copy(state.at[:, :, j], u.at[:, 2 + j], load_sem.at[j]) for j in range(4)]
    for copy in loads:
        copy.start()
    fetch = [
        pltpu.make_async_copy(transforms.at[a:b], to, table_sem.at[n])
        for n, (a, b, to) in enumerate(
            (
                (2048, 2048 + 2 * RANK, small),
                (2112, 2176, large),
                (0, 4 * MMAX * GROUPS, forth),
                (1024, 1024 + RANK * sectors, home_again.at[:, 0:128]),
                (1536, 1536 + RANK * sectors, home_again.at[:, 128:256]),
            )
        )
    ]

    barrier = pltpu.get_barrier_semaphore()

    def greet(b, a):
        pl.semaphore_signal(barrier, inc=1, device_id=(b, a), device_id_type=MESH)

    @pl.when(first)
    def _():
        greet(1, az)

        @pl.when(jnp.logical_not(apart))
        def _():
            for i in others:
                greet(0, at(i))

    @pl.when((blk == 1) & apart)
    def _():
        for i in others:
            greet(0, at(i))

    @pl.when(first)
    def _():
        for copy in fetch[:2]:
            copy.start()

    @pl.when(owner)
    def _():
        for copy in fetch[2:]:
            copy.start()

    @pl.when(blk > 0)
    def _():
        greet(blk - 1, az)
        greet(blk, at(1))
        greet(blk, at(sectors - 1))

        @pl.when(blk < blocks - 1)
        def _():
            greet(blk + 1, az)

    def remote(src, dst, send, recv, b, a):
        return pltpu.make_async_remote_copy(
            src_ref=src, dst_ref=dst, send_sem=send, recv_sem=recv, device_id=(b, a), device_id_type=MESH
        )

    up = remote(u.at[:, 4:6], u.at[:, 0:2], hs.at[0], hr.at[0], jnp.minimum(blk + 1, blocks - 1), az)
    down = remote(u.at[:, 2:4], u.at[:, 6:8], hs.at[1], hr.at[1], jnp.maximum(blk - 1, 0), az)
    ahead = remote(state.at[:, 62:64], halo.at[0], hs.at[2], hr.at[2], blk, at(1))
    behind = remote(state.at[:, 0:2], halo.at[1], hs.at[3], hr.at[3], blk, at(sectors - 1))

    dz[...] = axial_matrix()

    @pl.when(first)
    def _():
        zero = jnp.zeros((64, 128), jnp.float32)
        for f in range(FIELDS):
            for c in range(2):
                rf[f, c] = zero
            for j in range(4):
                gs[f, j, 0:16] = zero[:16]
                gs[f, j, 80:96] = zero[:16]
                sg[f, j, 72:80] = zero[:8]

    for copy in loads:
        copy.wait()

    @pl.when(blk > 0)
    def _():
        @pl.when(blk < blocks - 1)
        def _():
            pl.semaphore_wait(barrier, 4)

        @pl.when(last)
        def _():
            pl.semaphore_wait(barrier, 3)

        down.start()

        @pl.when(blk < blocks - 1)
        def _():
            up.start()

        ahead.start()
        behind.start()

    base = (blk * 4).astype(jnp.float32) + 0.5

    def radius(j):
        return base + float(j)

    def own(j):
        r = radius(j)
        rate = STEP / r
        for h in (0, 32):
            rows = slice(h, h + 32)
            q = [u[f, 2 + j, rows] for f in range(FIELDS)]
            ur, ut, uz, p = primitives(q)
            e = q[4] + p
            cross = q[1] * ut
            swirl = q[2] * ut + p
            radial = [q[1], q[1] * ur + p, cross, q[3] * ur, e * ur]
            azimuth = [q[2], cross, swirl, q[3] * ut, e * ut]
            axial = [q[3], q[1] * uz, q[2] * uz, q[3] * uz + p, e * uz]
            grown = [q[0], q[1] + rate * swirl, q[2] - rate * cross, q[3], q[4]]
            for f in range(FIELDS):
                rf[f, 2 + j, rows] = r * radial[f]
                gs[f, j, 16 + h : 48 + h] = azimuth[f]
                sb[f, j, rows] = grown[f]
                high, low = split(axial[f])
                hh[j, 64 * f + h : 64 * f + h + 32, 0:128] = high
                hh[j, 64 * f + h : 64 * f + h + 32, 128:256] = low
        zd[j] = product(hh[j], dz[...])

    def far_flux(c):
        r = base + float(c - 2)
        for h in (0, 32):
            rows = slice(h, h + 32)
            q = [u[f, c, rows] for f in range(FIELDS)]
            ur, _, _, p = primitives(q)
            radial = [q[1], q[1] * ur + p, q[2] * ur, q[3] * ur, (q[4] + p) * ur]
            for f in range(FIELDS):
                rf[f, c, rows] = r * radial[f]

    turn = STEP / (12.0 * 2.0 * math.pi / (64 * sectors))

    def slope_angle(f, j, start, count):
        def part(offset):
            return gs[f, j, start + 16 + offset : start + 16 + offset + count]

        return (part(-2) - part(2)) + 8.0 * (part(1) - part(-1))

    def advance(j):
        kr = (STEP / 12.0) / radius(j)
        kt = turn / radius(j)
        for f in range(FIELDS):
            for h in (0, 32):
                rows = slice(h, h + 32)
                rad = (rf[f, j, rows] - rf[f, j + 4, rows]) + 8.0 * (rf[f, j + 3, rows] - rf[f, j + 1, rows])
                sg[f, j, rows] = (
                    sb[f, j, rows] - kr * rad - kt * slope_angle(f, j, h, 32) - (STEP / 12.0) * zd[j, 64 * f + h : 64 * f + h + 32]
                )

    def edges(j):
        kt = turn / radius(j)
        for f in range(FIELDS):
            sg[f, j, 64:72] = -kt * (slope_angle(f, j, 64, 8) + slope_angle(f, j, -8, 8))

    def short(f, j, start, count):
        parts = product(small[:, 0:count], jnp.concatenate(split(sg[f, j, start : start + count]), 1))
        parts = parts[0:RANK] + parts[RANK : 2 * RANK]
        return parts[:, 0:128] + parts[:, 128:256]

    def pack(j):
        for f in range(FIELDS):
            sides = [short(f, j, 0, 80)] + ([short(f, j, 80, 64)] if j < 2 else [])
            for n, values in enumerate(sides):
                if f < 4:
                    yw[f, j, RANK * n : RANK * n + RANK] = values
                else:
                    groups = [values[8 * g : 8 * g + 8] for g in range(GROUPS)]
                    groups += [jnp.zeros((8, 128), jnp.float32)] * (4 - GROUPS)
                    for q, part in enumerate(exchanged(groups)):
                        pk[j, q, 8 * n : 8 * n + 8] = part

    def shifted(dx, dy):
        return lax.rem(y + dy, 4) * 4 + lax.rem(x + dx, 4)

    def home(target):
        return jnp.where(target == 0, 1, 0)

    def forward(target, slot, rows):
        f, j, _ = units_of(target)
        return remote(yw.at[f, j, 0:rows], rx.at[az, 0:rows], fs.at[0, slot], fr.at[0, az], home(target), target)

    def forward_quarter(target, slot, rows):
        q, _, j = units_of(target)
        return remote(pk.at[j, q, 0:rows], rq.at[az, 0:rows], fs.at[1, slot], fr.at[1, az], home(target), target)

    def forward_all(inner, act):
        for i, (dx, dy) in enumerate(OFFSETS + [(0, 0)]):
            target = shifted(dx, dy)
            whole = units_of(target)[1] < 2 if inner else units_of(target)[1] >= 2
            away = True if dx or dy else apart

            @pl.when(whole & away)
            def _():
                act(forward(target, i, 2 * RANK if inner else RANK))

            @pl.when(jnp.logical_not(whole) & away)
            def _():
                act(forward_quarter(target, i, 16 if inner else 8))

    my_f, my_j, my_quarter = units_of(az)
    my_inner = my_j < 2

    @pl.when(first)
    def _():
        for c in (4, 5):
            far_flux(c)
        for j in range(2):
            own(j)
        for copy in fetch[:2]:
            copy.wait()
        for j in range(2):
            advance(j)
            edges(j)
            kr = (STEP / 12.0) / radius(j)
            for f in range(FIELDS):
                inner = rf[f, 3] - 8.0 * rf[f, 2] if j == 0 else rf[f, 2]
                sg[f, j, 80:144] = (-SIGN[f] * kr) * inner
            pack(j)
        pl.semaphore_wait(barrier, sectors)
        forward_all(True, lambda c: c.start())
        up.start()
        for j in range(2, 4):
            own(j)

    @pl.when(blk > 0)
    def _():
        for j in range(4):
            own(j)
        ahead.wait_recv()
        behind.wait_recv()
        for side in range(2):
            for a in range(2):
                q = [halo[side, f, a] for f in range(FIELDS)]
                _, ut, _, p = primitives(q)
                azimuth = [q[2], q[1] * ut, q[2] * ut + p, q[3] * ut, (q[4] + p) * ut]
                row = (14 if side == 0 else 80) + a
                for f in range(FIELDS):
                    for j in range(4):
                        gs[f, j, row : row + 1] = azimuth[f][j : j + 1]
        up.wait_recv()
        for c in range(2):
            far_flux(c)

    @pl.when(last)
    def _():
        for f in range(FIELDS):
            for c in (6, 7):
                u[f, c] = u[f, 5]

    @pl.when(blk < blocks - 1)
    def _():
        down.wait_recv()

    for c in (6, 7):
        far_flux(c)

    def plain(j):
        return pltpu.make_async_copy(sg.at[:, j, 0:64], out.at[:, j], out_sem.at[0, j])

    @pl.when(first)
    def _():
        for j in range(2, 4):
            advance(j)
            edges(j)
            pack(j)
        forward_all(False, lambda c: c.start())

    @pl.when(blk > 0)
    def _():
        for j in range(4):
            advance(j)
            plain(j).start()

    def back(dx, dy):
        target = shifted(dx, dy)
        return remote(kp.at[target], zin.at[my_f, my_j], bs.at[0, 4 * dy + dx], br.at[0, az], 0, target)

    def back_quarter(dx, dy):
        target = shifted(dx, dy)
        return remote(kq.at[target], qin.at[my_quarter, my_f], bs.at[1, 4 * dy + dx], br.at[1, az], 0, target)

    @pl.when(owner)
    def _():
        for whole_inner in (True, False):
            rows, few = (2 * RANK, 8) if whole_inner else (RANK, 16)

            @pl.when(my_inner if whole_inner else jnp.logical_not(my_inner))
            def _(rows=rows, few=few):
                mine = [
                    pltpu.make_async_copy(yw.at[my_f, my_j, 0:rows], rx.at[az, 0:rows], own_sem.at[0]),
                    pltpu.make_async_copy(pk.at[my_quarter, my_f, 0:few], rq.at[az, 0:few], own_sem.at[1]),
                ]

                def arrived(s):
                    remote(yw.at[0, 0, 0:rows], rx.at[s, 0:rows], fs.at[0, 0], fr.at[0, s], 0, s).wait_recv()
                    remote(pk.at[0, 0, 0:few], rq.at[s, 0:few], fs.at[1, 0], fr.at[1, s], 0, s).wait_recv()

                @pl.when(first)
                def _():
                    for copy in mine:
                        copy.start()
                    for copy in mine:
                        copy.wait()

                @pl.when(blk > 0)
                def _():
                    arrived(az)

                for i in others:
                    arrived(at(i))

                group = lax.broadcasted_iota(jnp.int32, (16, 128), 1) // 32

                def gather(n, carry):
                    pair = (2 * n, 2 * n + 1)
                    across = [lax.rem(s + sectors // 2, sectors) for s in pair]
                    quarter = jnp.concatenate([rq[s, 0:8] for s in pair], 0)
                    if few == 16:
                        quarter = quarter + jnp.concatenate([rq[s, 8:16] for s in across], 0)
                    for g in range(GROUPS):
                        value = jnp.concatenate([rx[s, 8 * g : 8 * g + 8] for s in pair], 0)
                        if rows == 2 * RANK:
                            value = value + jnp.concatenate(
                                [rx[s, RANK + 8 * g : RANK + 8 * g + 8] for s in across], 0
                            )
                        to = pl.ds(pl.multiple_of(128 * g + n * 16, 16), 16)
                        high, low = split(value)
                        xs[to, 0:128] = high
                        xs[to, 128:256] = low
                        high, low = split(jnp.where(group == g, quarter, 0.0))
                        xs[to, 256:384] = high
                        xs[to, 384:512] = low
                    return carry

                lax.fori_loop(0, sectors // 2, gather, 0, unroll=8)

        for copy in fetch[2:]:
            copy.wait()
        order = lax.rem(lax.broadcasted_iota(jnp.int32, (2 * MMAX, 128), 0), MMAX)
        scale = jnp.where(order == 0, 1.0, 2.0) / float(64 * sectors)
        sides = []
        for n, cycle in ((0, my_j), (256, my_quarter)):
            parts = product(forth[0:256], xs[0:128, n : n + 256])
            for g in range(1, GROUPS):
                parts = parts + product(
                    forth[256 * g : 256 * g + 256], xs[128 * g : 128 * g + 128, n : n + 256]
                )
            parts = parts[0:128] + parts[128:256]
            coef = parts[:, 0:128] + parts[:, 128:256]
            if n:
                coef = coef + pltpu.roll(coef, 64, 1)
                coef = coef + pltpu.roll(coef, 32, 1)
            sides.extend(split(coef * jnp.where(order < cut[cycle], scale, 0.0)))
        both = jnp.concatenate(sides, 1)
        both = jnp.concatenate([both, both], 0)
        group = lax.broadcasted_iota(jnp.int32, (8, 128), 1) // 32
        for dy in (2, 1, 3, 0):
            yy = lax.rem(y + dy, 4)
            kept = product(home_again[pl.ds(pl.multiple_of(yy * 4 * RANK, 4 * RANK), 4 * RANK)], both)
            whole = kept[:, 0:128] + kept[:, 128:256]
            part = kept[:, 256:384] + kept[:, 384:512]
            for i in range(4):
                kp[yy * 4 + i] = whole[RANK * i : RANK * i + RANK]
                packed = part[RANK * i : RANK * i + 8]
                for g in range(1, GROUPS):
                    packed = jnp.where(group == g, part[RANK * i + 8 * g : RANK * i + 8 * g + 8], packed)
                kq[yy * 4 + i] = packed
            for dx in (2, 1, 3, 0):
                if dx or dy:
                    back_quarter(dx, dy).start()
                    back(dx, dy).start()

        @pl.when(blk > 0)
        def _():
            back_quarter(0, 0).start()
            back(0, 0).start()

        @pl.when(first)
        def _():
            mine = [
                pltpu.make_async_copy(kp.at[az], zin.at[my_f, my_j], own_sem.at[0]),
                pltpu.make_async_copy(kq.at[az], qin.at[my_quarter, my_f], own_sem.at[1]),
            ]
            for copy in mine:
                copy.start()
            for copy in mine:
                copy.wait()

    @pl.when(first)
    def _():
        def quarter_back(o):
            q, _, j = units_of(o)
            remote(kq.at[0], qin.at[j, q], bs.at[1, 0], br.at[1, o], home(o), o).wait_recv()

        def whole_back(o):
            f, j, _ = units_of(o)
            remote(kp.at[0], zin.at[f, j], bs.at[0, 0], br.at[0, o], home(o), o).wait_recv()

        def full(f, j, values):
            both = jnp.concatenate(split(jnp.concatenate([values, values], 0)), 1)
            parts = product(large[:, 0 : 2 * RANK], both)
            sg[f, j, 0:64] = parts[:, 0:128] + parts[:, 128:256]

        for i in others:
            quarter_back(at(i))

        @pl.when(apart)
        def _():
            quarter_back(az)
            whole_back(az)

        for j in range(4):
            full(4, j, jnp.concatenate(exchanged([qin[j, q] for q in range(4)])[:GROUPS], 0))
        for i in others:
            whole_back(at(i))
        for j in range(4):
            for f in range(4):
                full(f, j, zin[f, j])
            plain(j).start()
        for j in range(4):
            plain(j).wait()
        up.wait_send()
        forward_all(True, lambda c: c.wait_send())
        forward_all(False, lambda c: c.wait_send())

    @pl.when(owner)
    def _():
        for dx, dy in OFFSETS:
            back(dx, dy).wait_send()
            back_quarter(dx, dy).wait_send()

        @pl.when(blk > 0)
        def _():
            back(0, 0).wait_send()
            back_quarter(0, 0).wait_send()

    @pl.when(blk > 0)
    def _():
        for j in range(4):
            plain(j).wait()
        down.wait_send()

        @pl.when(blk < blocks - 1)
        def _():
            up.wait_send()

        ahead.wait_send()
        behind.wait_send()


def place(held, out, sems):
    copies = [pltpu.make_async_copy(held.at[:, j], out.at[:, :, j], sems.at[j]) for j in range(4)]
    for copy in copies:
        copy.start()
    for copy in copies:
        copy.wait()


def shards(cut_table, blocks, sectors, state, cutoffs):
    points = state.shape[3]
    f32, bf16 = jnp.float32, jnp.bfloat16
    dma = pltpu.SemaphoreType.DMA
    anywhere = pl.BlockSpec(memory_space=pl.ANY)
    held = pl.pallas_call(
        functools.partial(kernel, blocks, sectors),
        out_shape=jax.ShapeDtypeStruct((FIELDS, 4, 64, points), f32),
        in_specs=[pl.BlockSpec(memory_space=pltpu.SMEM)] + [anywhere] * 2,
        out_specs=anywhere,
        scratch_shapes=[
            pltpu.VMEM((FIELDS, 8, 64, points), f32),
            pltpu.VMEM((FIELDS, 8, 64, points), f32),
            pltpu.VMEM((FIELDS, 4, 96, points), f32),
            pltpu.VMEM((4, FIELDS * 64, 2 * points), bf16),
            pltpu.VMEM((4, FIELDS * 64, points), f32),
            pltpu.VMEM((FIELDS, 4, 64, points), f32),
            pltpu.VMEM((FIELDS, 4, 144, points), f32),
            pltpu.VMEM((2, FIELDS, 2, 4, points), f32),
            pltpu.VMEM((4, 4, 2 * RANK, points), f32),
            pltpu.VMEM((sectors, 2 * RANK, points), f32),
            pltpu.VMEM((sectors, 16, points), f32),
            pltpu.VMEM((4, 4, 16, points), f32),
            pltpu.VMEM((RANK * sectors, 4 * points), bf16),
            pltpu.VMEM((sectors, RANK, points), f32),
            pltpu.VMEM((sectors, 8, points), f32),
            pltpu.VMEM((4, 4, 8, points), f32),
            pltpu.VMEM((4, 4, RANK, points), f32),
            pltpu.VMEM((2 * RANK, 128), bf16),
            pltpu.VMEM((64, 128), bf16),
            pltpu.VMEM((4 * MMAX * GROUPS, 128), bf16),
            pltpu.VMEM((RANK * sectors, 4 * MMAX), bf16),
            pltpu.VMEM((2 * points, points), bf16),
            dma((4,)),
            dma((5,)),
            dma((4,)),
            dma((4,)),
            dma((2, sectors)),
            dma((2, sectors)),
            dma((2, sectors)),
            dma((2, sectors)),
            dma((2,)),
            dma((FIELDS, 4)),
        ],
        compiler_params=pltpu.CompilerParams(
            collective_id=0, has_side_effects=True, vmem_limit_bytes=LIMIT_MIB * 1024 * 1024
        ),
        name="section",
    )(cutoffs, state, jnp.asarray(cut_table))
    return pl.pallas_call(
        place,
        out_shape=jax.ShapeDtypeStruct(state.shape, f32),
        in_specs=[anywhere],
        out_specs=anywhere,
        scratch_shapes=[dma((4,))],
        compiler_params=pltpu.CompilerParams(vmem_limit_bytes=1024 * 1024),
        name="place",
    )(held)


def solution(mesh):
    blocks, sectors = mesh.shape["blk"], mesh.shape["az"]
    placed = (P(None, "az", "blk", None), P())
    return jax.shard_map(
        functools.partial(shards, tables(64 * sectors), blocks, sectors),
        mesh=mesh,
        in_specs=placed,
        out_specs=P(None, "az", "blk", None),
        check_vma=False,
    )
```
